32 devices in a mesh: shot: 4 (over y, x), tile: 8 (over z, core).
Axes of the slice: x: 2, y: 2, z: 4, core: 2. Of those that a mesh axis runs over, the one named last changes fastest.
Arguments:
- src_field: bfloat16 [4, 6, 3, 64, 8, 1024], P('shot', None, None, 'tile'), may hold values from -2.5 to 2.5
- rcv_field: bfloat16 [4, 6, 3, 64, 8, 1024], P('shot', None, None, 'tile'), may hold values from -2.5 to 2.5
- model_panels: bfloat16 [64, 3, 8, 1024], P('tile'), may hold values from 1 to 3
- deriv_taps: float32 [3, 16], replicated, may hold values from -0.25 to 0.25
- aperture: int32 [4, 64], replicated, may hold values from 0 to 63, as said below
- tile_slot: int32 [64], replicated, may hold values from 0 to 63, as said below
Outputs:
- gradient: float32 [64, 4, 8, 1024], P('tile', None, None, 'shot')
The draws below stay inside these ranges and needn't reach their ends.
Inputs may be any that keep to these rules, and one draw needn't show every extreme that they name: `aperture`: positions t*8 to t*8 + 7 of a row name 8 distinct tiles for device t; their storage rows lie on exactly 6 distinct tile devices (storage row // 8), at most 2 on any one, and exactly 2 on 2 of them for every device. A permutation: tile m is stored in row tile_slot[m] of model_panels and gradient.
All inputs are finite; a program needn't handle non-finite values.
Results may differ from the reference program's by a relative error of at most 0.0049.
Values may be sent and summed in bfloat16 or wider, within the bound.
A program may use at most 320 MiB of HBM per device.

```python
import jax
import jax.numpy as jnp
from jax import lax

PX = 8
PY = 8
NZ = 128
LEVELS = 6
TAPS = 16
MT_DEV = 8
GROUPS = 4
PANELS = 8
MT = 64
N_TILE = 8


def request_plan(key):
    base = jax.random.fold_in(key, 11)
    storage = jax.random.permutation(jax.random.fold_in(base, 1), MT).astype(jnp.int32)
    owner_ids = jnp.arange(PANELS, dtype=jnp.int32)
    scores = jax.random.randint(jax.random.fold_in(base, 2), (GROUPS, PANELS, PANELS), 0, 2 * PANELS, dtype=jnp.int32)
    priority = (scores + owner_ids) * PANELS + owner_ids
    order = jnp.argsort(priority, axis=-1, stable=True).astype(jnp.int32)
    double = PANELS // 4
    single = PANELS - double
    owners = jnp.concatenate([order[..., :single], order[..., :double]], axis=-1)
    first = jax.random.randint(jax.random.fold_in(base, 3), (GROUPS, PANELS, single), 0, MT_DEV, dtype=jnp.int32)
    further = jax.random.randint(jax.random.fold_in(base, 4), (GROUPS, PANELS, double), 0, MT_DEV - 1, dtype=jnp.int32)
    second = (first[..., :double] + 1 + further) % MT_DEV
    within = jnp.concatenate([first, second], axis=-1)
    slot_ids = owners * MT_DEV + within
    mixing = jax.random.randint(jax.random.fold_in(base, 5), (GROUPS, PANELS, PANELS), 0, 1 << 20, dtype=jnp.int32)
    mixing = mixing * PANELS + jnp.arange(PANELS, dtype=jnp.int32)
    positions = jnp.argsort(mixing, axis=-1, stable=True).astype(jnp.int32)
    slot_ids = jnp.take_along_axis(slot_ids, positions, axis=-1)
    inverse = jnp.zeros((MT,), jnp.int32).at[storage].set(jnp.arange(MT, dtype=jnp.int32))
    tile_ids = inverse[slot_ids].reshape(GROUPS, PANELS * PANELS)
    return (tile_ids, storage)


def draw_aperture(key, part):
    tile_ids, storage = request_plan(key)
    return tile_ids


def draw_tile_slot(key, part):
    tile_ids, storage = request_plan(key)
    return storage


def steps_of(stream_key, dims, split, smallest, high):
    def one(position, blocks):
        draws = jax.random.uniform(jax.random.fold_in(jax.random.fold_in(stream_key, 6), position), (blocks,), jnp.float32, smallest / len(split), high / len(split))
        return jnp.repeat(jnp.exp(draws), dims[position] // blocks).reshape((-1,) + (1,) * (len(dims) - position - 1))

    loudness = one(*split[0])
    for cut in split[1:]:
        loudness = loudness * one(*cut)
    return loudness


def gaussian(key, dims, spread, bound, shards=(), kind=jnp.bfloat16):
    level = steps_of(key, dims, shards, -0.22, 0.18) if shards else 1.0
    entries = jax.random.normal(key, dims, jnp.float32) * spread * level
    return jnp.minimum(jnp.maximum(entries, -bound), bound).astype(kind)


def setup_inputs(seed: int = 0) -> dict:
    streams_of = jax.random.split(jax.random.key(seed), 7)
    return {
        "src_field": gaussian(streams_of[0], (GROUPS, LEVELS, 3, N_TILE * PANELS, PX, PY * NZ), 0.3, 2.5, ((0, 4), (3, 8))),
        "rcv_field": gaussian(streams_of[1], (GROUPS, LEVELS, 3, N_TILE * PANELS, PX, PY * NZ), 0.3, 2.5, ((0, 4), (3, 8))),
        "model_panels": jnp.clip(1.0 + 2.0 * jax.random.uniform(streams_of[2], (MT, 3, PX, PY * NZ), jnp.float32) ** steps_of(streams_of[2], (MT, 3, PX, PY * NZ), ((0, 8),), -0.2, 0.2), 1.0, 3.0).astype(jnp.bfloat16),
        "deriv_taps": jnp.clip(jax.random.uniform(streams_of[3], (3, TAPS), jnp.float32, -0.25, 0.25), -0.25, 0.25),
        "aperture": draw_aperture(jax.random.fold_in(streams_of[6], 71), 0),
        "tile_slot": draw_tile_slot(jax.random.fold_in(streams_of[6], 71), 0),
    }


def tap_matrix(taps_row, length):
    rows_at = jnp.arange(length, dtype=jnp.int32)[:, None]
    cols_at = jnp.arange(length, dtype=jnp.int32)[None, :]
    offset = rows_at - cols_at + TAPS // 2
    match = offset[:, :, None] == jnp.arange(TAPS, dtype=jnp.int32)[None, None, :]
    return jnp.sum(jnp.where(match, taps_row[None, None, :], 0.0), axis=-1).astype(jnp.bfloat16)


def derivatives(field, filters):
    filter_x, filter_y, filter_z = [mat.astype(jnp.float32) for mat in filters]
    wide = field.astype(jnp.float32)
    deriv_z = jnp.einsum("ckxyz,zw->ckxyw", wide, filter_z)
    deriv_y = jnp.einsum("ckxyz,yw->ckxwz", wide, filter_y)
    deriv_x = jnp.einsum("ckxyz,xw->ckwyz", wide, filter_x)
    divergence = deriv_x[0] + deriv_y[1] + deriv_z[2]
    curl = (deriv_y[2] - deriv_z[1], deriv_z[0] - deriv_x[2], deriv_x[1] - deriv_y[0])
    return divergence, curl


def panel_terms(source, receiver, panels, filters):
    panel_count = source.shape[2]
    shape_in = (3, panel_count, PX, PY, NZ)
    image_pp = jnp.zeros((panel_count, PX, PY, NZ), jnp.float32)
    image_ps, image_sp, image_ss = image_pp, image_pp, image_pp
    for level_index in range(LEVELS):
        div_src, curl_src = derivatives(source[level_index].reshape(shape_in), filters)
        div_rcv, curl_rcv = derivatives(receiver[level_index].reshape(shape_in), filters)
        image_pp = image_pp + div_src * div_rcv
        image_ps = image_ps + div_src * (curl_rcv[0] + curl_rcv[1] + curl_rcv[2])
        image_sp = image_sp + (curl_src[0] + curl_src[1] + curl_src[2]) * div_rcv
        image_ss = image_ss + curl_src[0] * curl_rcv[0] + curl_src[1] * curl_rcv[1] + curl_src[2] * curl_rcv[2]
    params = panels.astype(jnp.float32).reshape(panel_count, 3, PX, PY, NZ)
    speed_p, speed_s, density = params[:, 0], params[:, 1], params[:, 2]
    stacked = jnp.stack([density * speed_p * image_pp, density * speed_s * image_ps,
                         density * speed_s * image_sp, density * speed_s * speed_s / speed_p * image_ss], axis=1)
    return stacked.reshape(panel_count, 4, PX, PY * NZ)


def reference(src_field, rcv_field, model_panels, deriv_taps, aperture, tile_slot):
    filters = (tap_matrix(deriv_taps[0], PX), tap_matrix(deriv_taps[1], PY), tap_matrix(deriv_taps[2], NZ))
    zero = jnp.int32(0)

    def one_device(accumulated, flat_index):
        group_id = (flat_index // N_TILE).astype(jnp.int32)
        tile_id = (flat_index % N_TILE).astype(jnp.int32)
        start = (tile_id * PANELS).astype(jnp.int32)
        source = lax.dynamic_slice(src_field, (group_id, zero, zero, start, zero, zero),
                                   (1, LEVELS, 3, PANELS, PX, PY * NZ))[0]
        receiver = lax.dynamic_slice(rcv_field, (group_id, zero, zero, start, zero, zero),
                                     (1, LEVELS, 3, PANELS, PX, PY * NZ))[0]
        tile_ids = lax.dynamic_slice(aperture, (group_id, start), (1, PANELS))[0]
        slot_ids = tile_slot[tile_ids]
        panels = model_panels[slot_ids]
        terms = panel_terms(source, receiver, panels, filters)
        return accumulated.at[slot_ids].add(terms), None

    initial = jnp.zeros((MT, 4, PX, PY * NZ), jnp.float32)
    summed, _ = lax.scan(one_device, initial, jnp.arange(GROUPS * N_TILE, dtype=jnp.int32))
    return summed
```

```python
import functools

import jax
import jax.numpy as jnp
from jax import lax
from jax.experimental import pallas as pl
from jax.experimental.pallas import tpu as pltpu
from jax.sharding import PartitionSpec as P

MESH = pl.DeviceIdType.MESH
TAPS = 16
NZ = 128
HALVES = 4


def tap_values(taps, axis, offset):
    total = jnp.zeros(offset.shape, jnp.float32)
    for tap in range(TAPS):
        total = jnp.where(offset == tap, taps[axis, tap], total)
    return total


def build_filters(taps, lateral, depth):
    rows = lax.broadcasted_iota(jnp.int32, (64, 64), 0)
    cols = lax.broadcasted_iota(jnp.int32, (64, 64), 1)
    same_y = (rows // 8) == (cols // 8)
    same_x = (rows % 8) == (cols % 8)
    along_x = jnp.where(same_y, tap_values(taps, 0, cols % 8 - rows % 8 + 8), 0.0)
    along_y = jnp.where(same_x, tap_values(taps, 1, cols // 8 - rows // 8 + 8), 0.0)
    none = jnp.zeros((64, 64), jnp.float32)
    table = (
        (along_x, along_y, none),
        (none, none, along_y),
        (none, none, -along_x),
        (-along_y, along_x, none),
    )
    for out, line in enumerate(table):
        lateral[out * 64 : out * 64 + 64, :] = jnp.concatenate(line, axis=1).astype(jnp.bfloat16)
    rows = lax.broadcasted_iota(jnp.int32, (NZ, NZ), 0)
    cols = lax.broadcasted_iota(jnp.int32, (NZ, NZ), 1)
    along_z = tap_values(taps, 2, rows - cols + 8).astype(jnp.bfloat16)
    zeros = jnp.zeros((NZ, NZ), jnp.bfloat16)
    depth[:NZ, :NZ] = along_z
    depth[:NZ, NZ:] = zeros
    depth[NZ:, :NZ] = zeros
    depth[NZ:, NZ:] = along_z


def kernel(shots, tiles, taps_far, aperture_far, tile_slot_far, src, rcv, model_far, out, fields, lateral, depth, images, gathered,
           pair_out, pair_in, line_out, line_in, load_sem, shot_send, shot_recv, pair_send, pair_recv,
           line_send, line_recv, table_vector, table, table_sem,
           taps, aperture, tile_slot, model, near_sem):
    s = lax.axis_index("shot")
    t = lax.axis_index("tile")
    chips = tiles // 2
    z, core = t // 2, t % 2
    partner = t + 1 - 2 * core
    panels, levels = fields.shape[1], fields.shape[2]
    owned = out.shape[0]
    part = owned // HALVES
    slots = tiles * owned

    def load(f, k):
        return pltpu.make_async_copy((src, rcv)[f].at[:, :, k], fields.at[f, k], load_sem.at[f, k])

    near = [
        pltpu.make_async_copy(far, ref, near_sem.at[i])
        for i, (far, ref) in enumerate(
            ((taps_far, taps), (aperture_far, aperture), (tile_slot_far, tile_slot), (model_far, model))
        )
    ]
    for copy in near:
        copy.start()

    @pl.loop(0, panels)
    def _(k):
        load(0, k).start()
        load(1, k).start()

    barrier = pltpu.get_barrier_semaphore()
    for d in range(1, shots):
        pl.semaphore_signal(barrier, inc=1, device_id=(lax.rem(s + d, shots), t), device_id_type=MESH)
    pl.semaphore_signal(barrier, inc=1, device_id=(s, partner), device_id_type=MESH)

    @pl.when(z > 0)
    def _():
        pl.semaphore_signal(barrier, inc=1, device_id=(s, t - 2), device_id_type=MESH)

    @pl.when(z < chips - 1)
    def _():
        pl.semaphore_signal(barrier, inc=1, device_id=(s, t + 2), device_id_type=MESH)

    near[0].wait()
    build_filters(taps, lateral, depth)
    near[1].wait()
    near[2].wait()
    slot_at = lax.broadcasted_iota(jnp.int32, (1, slots), 1)
    for g in range(shots):
        found = jnp.full((1, slots), panels, jnp.int32)
        for k in range(panels):
            found = jnp.where(slot_at == tile_slot[aperture[g, t * panels + k]], k, found)
        table_vector[g : g + 1, :] = found
    table_copy = pltpu.make_async_copy(table_vector, table, table_sem)
    table_copy.start()
    for g in range(shots):
        gathered[g, panels] = jnp.zeros(gathered.shape[2:], gathered.dtype)

    @pl.when(z == 0)
    def _():
        @pl.loop(0, chips)
        def _(block):
            line_in[0, block] = jnp.zeros(line_in.shape[2:], line_in.dtype)

    @pl.when(z == chips - 1)
    def _():
        @pl.loop(0, chips)
        def _(block):
            line_in[1, block] = jnp.zeros(line_in.shape[2:], line_in.dtype)

    def shot_copy(d, k):
        peer = lax.rem(s + d, shots)
        return pltpu.make_async_remote_copy(
            src_ref=images.at[peer, k],
            dst_ref=gathered.at[s, k],
            send_sem=shot_send.at[d - 1, k],
            recv_sem=shot_recv.at[d - 1, k],
            device_id=(peer, t),
            device_id_type=MESH,
        )

    def parts(f, k, j):
        left = fields[f, k, 2 * j].reshape(192, NZ)
        right = fields[f, k, 2 * j + 1].reshape(192, NZ)
        both = jnp.concatenate([left, right], axis=1)
        flat = jnp.dot(lateral[...], both, preferred_element_type=jnp.float32)
        deep = jnp.dot(both, depth[...], preferred_element_type=jnp.float32)
        return (
            flat[0:64] + deep[128:192],
            flat[64:128] - deep[64:128],
            flat[128:192] + deep[0:64],
            flat[192:256],
        )

    @pl.loop(0, panels, unroll=2)
    def _(k):
        load(0, k).wait()
        load(1, k).wait()
        sums = None
        for j in range(levels // 2):
            a, a0, a1, a2 = parts(0, k, j)
            b, b0, b1, b2 = parts(1, k, j)
            new = (a * b, a * (b0 + b1 + b2), (a0 + a1 + a2) * b, a0 * b0 + a1 * b1 + a2 * b2)
            sums = new if sums is None else tuple(x + y for x, y in zip(sums, new))
        for c in range(4):
            image = (sums[c][:, :NZ] + sums[c][:, NZ:]).astype(jnp.bfloat16)
            images[:, k, c] = image.reshape(shots, 64 // shots, NZ)
        gathered[s, k] = images[s, k]

        @pl.when(k == 0)
        def _():
            pl.semaphore_wait(barrier, shots + jnp.where(z > 0, 1, 0) + jnp.where(z < chips - 1, 1, 0))

        for d in range(1, shots):
            shot_copy(d, k).start()

    @pl.loop(0, panels)
    def _(k):
        for d in range(1, shots):
            shot_copy(d, k).wait_recv()

    table_copy.wait()
    near[3].wait()

    def combined(row):
        total = gathered[0, table[0, row]].astype(jnp.float32)
        for g in range(1, shots):
            total = total + gathered[g, table[g, row]].astype(jnp.float32)
        return total

    def pair_copy(block, h):
        return pltpu.make_async_remote_copy(
            src_ref=pair_out.at[block, h],
            dst_ref=pair_in.at[block, h],
            send_sem=pair_send.at[block, h],
            recv_sem=pair_recv.at[block, h],
            device_id=(s, partner),
            device_id_type=MESH,
        )

    @pl.loop(0, chips)
    def _(i):
        block = jnp.where(i % 2 == 0, chips - 1 - i // 2, i // 2)
        for h in range(HALVES):
            base = (2 * block + 1 - core) * owned + h * part

            for r in range(part):
                pair_out[block, h, r] = combined(base + r).astype(jnp.bfloat16)

            pair_copy(block, h).start()

    def line_copy(way, block, h):
        return pltpu.make_async_remote_copy(
            src_ref=line_out.at[block, h],
            dst_ref=line_in.at[way, block, h],
            send_sem=line_send.at[block, h],
            recv_sem=line_recv.at[way, block, h],
            device_id=(s, t + 2 - 4 * way),
            device_id_type=MESH,
        )

    def onward(way, block):
        has = jnp.where(way == 0, z < block, z > block)
        first = jnp.where(way == 0, z == 0, z == chips - 1)

        @pl.when(has)
        def _():
            for h in range(HALVES):
                pair_copy(block, h).wait_recv()

                @pl.when(jnp.logical_not(first))
                def _():
                    line_copy(way, block, h).wait_recv()

                base = (2 * block + core) * owned + h * part
                for r in range(part):
                    total = combined(base + r) + pair_in[block, h, r].astype(jnp.float32)
                    total = total + line_in[way, block, h, r].astype(jnp.float32)
                    line_out[block, h, r] = total.astype(jnp.bfloat16)
                line_copy(way, block, h).start()

    lead = jnp.where(z < chips // 2, 0, 1)

    @pl.loop(0, chips - 1)
    def _(i):
        for turn in range(2):
            way = lead if turn == 0 else 1 - lead
            onward(way, jnp.where(way == 0, chips - 1 - i, i))

    width = 64 // shots
    for h in range(HALVES):
        pair_copy(z, h).wait_recv()

        @pl.when(z > 0)
        def _():
            line_copy(0, z, h).wait_recv()

        @pl.when(z < chips - 1)
        def _():
            line_copy(1, z, h).wait_recv()

        base = t * owned + h * part
        for r in range(part):
            total = combined(base + r) + pair_in[z, h, r].astype(jnp.float32)
            total = total + line_in[0, z, h, r].astype(jnp.float32)
            total = total + line_in[1, z, h, r].astype(jnp.float32)
            row = h * part + r
            rows = pl.ds(pl.multiple_of(s * width, width), width)
            speed_p = model[row, 0, rows].astype(jnp.float32)
            speed_s = model[row, 1, rows].astype(jnp.float32)
            density = model[row, 2, rows].astype(jnp.float32)
            out[row, 0] = density * speed_p * total[0]
            out[row, 1] = density * speed_s * total[1]
            out[row, 2] = density * speed_s * total[2]
            out[row, 3] = density * speed_s * speed_s / speed_p * total[3]

    @pl.loop(0, panels)
    def _(k):
        for d in range(1, shots):
            shot_copy(d, k).wait_send()

    @pl.loop(0, chips)
    def _(block):
        for h in range(HALVES):
            pair_copy(block, h).wait_send()

        @pl.when(block != z)
        def _():
            for h in range(HALVES):
                line_copy(0, block, h).wait_send()


def tall(array):
    lead = array.shape[:-2]
    wide = array.shape[-1] // NZ
    array = array.reshape(lead + (8, wide, NZ))
    return jnp.swapaxes(array, -3, -2).reshape(lead + (8 * wide, NZ))


def body(src_field, rcv_field, model_panels, deriv_taps, aperture, tile_slot):
    tiles = lax.axis_size("tile")
    shots = lax.axis_size("shot")
    owned = model_panels.shape[0]
    panels, levels = src_field.shape[3], src_field.shape[1]
    chips = tiles // 2
    slots = tiles * owned
    part = owned // HALVES
    width = 64 // shots

    vmem = pl.BlockSpec(memory_space=pltpu.VMEM)
    hbm = pl.BlockSpec(memory_space=pltpu.HBM)
    half = (part, 4, width, NZ)
    half_sem = pltpu.SemaphoreType.DMA((chips, HALVES))
    result = pl.pallas_call(
        functools.partial(kernel, shots, tiles),
        out_shape=pltpu.VMEM((owned, 4, width, NZ), jnp.float32),
        in_specs=[hbm] * 6,
        out_specs=vmem,
        scratch_shapes=[
            pltpu.VMEM((2, panels, levels, 3, 64, NZ), jnp.bfloat16),
            pltpu.VMEM((256, 192), jnp.bfloat16),
            pltpu.VMEM((2 * NZ, 2 * NZ), jnp.bfloat16),
            pltpu.VMEM((shots, panels, 4, width, NZ), jnp.bfloat16),
            pltpu.VMEM((shots, panels + 1, 4, width, NZ), jnp.bfloat16),
            pltpu.VMEM((chips, HALVES) + half, jnp.bfloat16),
            pltpu.VMEM((chips, HALVES) + half, jnp.bfloat16),
            pltpu.VMEM((chips, HALVES) + half, jnp.bfloat16),
            pltpu.VMEM((2, chips, HALVES) + half, jnp.bfloat16),
            pltpu.SemaphoreType.DMA((2, panels)),
            pltpu.SemaphoreType.DMA((shots - 1, panels)),
            pltpu.SemaphoreType.DMA((shots - 1, panels)),
            half_sem,
            half_sem,
            half_sem,
            pltpu.SemaphoreType.DMA((2, chips, HALVES)),
            pltpu.VMEM((shots, slots), jnp.int32),
            pltpu.SMEM((shots, slots), jnp.int32),
            pltpu.SemaphoreType.DMA,
            pltpu.SMEM(deriv_taps.shape, jnp.float32),
            pltpu.SMEM(aperture.shape, jnp.int32),
            pltpu.SMEM(tile_slot.shape, jnp.int32),
            pltpu.VMEM((owned, 3, 64, NZ), jnp.bfloat16),
            pltpu.SemaphoreType.DMA((4,)),
        ],
        compiler_params=pltpu.CompilerParams(collective_id=0, has_side_effects=True, vmem_limit_bytes=48 * 1024 * 1024),
    )(*[pltpu.with_memory_space_constraint(v, pltpu.HBM) for v in (deriv_taps, aperture, tile_slot, tall(src_field[0]), tall(rcv_field[0]), tall(model_panels))])

    def spill(near, far, sem):
        copies = [pltpu.make_async_copy(near.at[r], far.at[r], sem.at[r]) for r in range(owned)]
        for copy in copies:
            copy.start()
        for copy in copies:
            copy.wait()

    wide = jnp.swapaxes(result.reshape(owned, 4, width // 8, 8, NZ), 2, 3)
    return wide.reshape(owned, 4, 8, (width // 8) * NZ)


def solution(mesh):
    return jax.shard_map(
        body,
        mesh=mesh,
        in_specs=(
            P("shot", None, None, "tile", None, None),
            P("shot", None, None, "tile", None, None),
            P("tile", None, None, None),
            P(),
            P(),
            P(),
        ),
        out_specs=P("tile", None, None, "shot"),
        check_vma=False,
    )
```

```python
import functools

import jax
import jax.numpy as jnp
from jax import lax
from jax.experimental import pallas as pl
from jax.experimental.pallas import tpu as pltpu
from jax.sharding import PartitionSpec as P

MESH = pl.DeviceIdType.MESH
TAPS = 16
NZ = 128
BATCH = 4


def tap_values(taps, axis, offset):
    total = jnp.zeros(offset.shape, jnp.float32)
    for tap in range(TAPS):
        total = jnp.where(offset == tap, taps[axis, tap], total)
    return total


def build_filters(taps, lateral, depth):
    rows = lax.broadcasted_iota(jnp.int32, (64, 64), 0)
    cols = lax.broadcasted_iota(jnp.int32, (64, 64), 1)
    same_y = (rows // 8) == (cols // 8)
    same_x = (rows % 8) == (cols % 8)
    along_x = jnp.where(same_y, tap_values(taps, 0, cols % 8 - rows % 8 + 8), 0.0)
    along_y = jnp.where(same_x, tap_values(taps, 1, cols // 8 - rows // 8 + 8), 0.0)
    none = jnp.zeros((64, 64), jnp.float32)
    table = (
        (along_x, along_y, none),
        (none, none, along_y),
        (none, none, -along_x),
        (-along_y, along_x, none),
    )
    for out, line in enumerate(table):
        lateral[out * 64 : out * 64 + 64, :] = jnp.concatenate(line, axis=1).astype(jnp.bfloat16)
    rows = lax.broadcasted_iota(jnp.int32, (NZ, NZ), 0)
    cols = lax.broadcasted_iota(jnp.int32, (NZ, NZ), 1)
    along_z = tap_values(taps, 2, rows - cols + 8).astype(jnp.bfloat16)
    zeros = jnp.zeros((NZ, NZ), jnp.bfloat16)
    depth[:NZ, :NZ] = along_z
    depth[:NZ, NZ:] = zeros
    depth[NZ:, :NZ] = zeros
    depth[NZ:, NZ:] = along_z


def kernel(shots, tiles, taps_far, aperture_far, tile_slot_far, src, rcv, model_far, out, fields, lateral, depth, images, gathered_first, gathered_second,
           line_out, relay_in, final_in, own_out, own_in, load_sem, shot_send, shot_recv, relay_send, relay_recv,
           final_send, final_recv, own_send, own_recv, table_vector, table, table_sem,
           taps, aperture, tile_slot, model, near_sem, factor):
    s = lax.axis_index("shot")
    t = lax.axis_index("tile")
    chips = tiles // 2
    z, core = t // 2, t % 2
    even = z % 2 == 0
    buddy = z + 1 - 2 * (z % 2)
    partner = t + 1 - 2 * core
    panels, levels = fields.shape[1], fields.shape[2]
    owned = out.shape[0]
    slots = tiles * owned
    width = 64 // shots
    gathered = (gathered_first, gathered_second)

    def load(f, k):
        return pltpu.make_async_copy((src, rcv)[f].at[:, :, k], fields.at[f, k], load_sem.at[f, k])

    near = [
        pltpu.make_async_copy(far, ref, near_sem.at[i])
        for i, (far, ref) in enumerate(
            ((taps_far, taps), (aperture_far, aperture), (tile_slot_far, tile_slot), (model_far, model))
        )
    ]
    near[0].start()

    @pl.loop(0, panels)
    def _(k):
        load(0, k).start()
        load(1, k).start()

    for copy in near[1:]:
        copy.start()

    def meets(other):
        apart = jnp.where(other > z, jnp.logical_or(z % 2 == 1, other % 2 == 0), jnp.logical_or(even, other % 2 == 1))
        return jnp.logical_and(other != z, jnp.logical_or(other == buddy, apart))

    barrier = pltpu.get_barrier_semaphore()
    expected = 2 * (shots - 1) + 1
    for d in range(1, shots):
        for h in range(2):
            pl.semaphore_signal(barrier, inc=1, device_id=(lax.rem(s + d, shots), 2 * z + h), device_id_type=MESH)
    pl.semaphore_signal(barrier, inc=1, device_id=(s, partner), device_id_type=MESH)
    for other in range(chips):
        expected = expected + jnp.where(meets(other), 2, 0)

        @pl.when(meets(other))
        def _():
            for h in range(2):
                pl.semaphore_signal(barrier, inc=1, device_id=(s, 2 * other + h), device_id_type=MESH)

    near[0].wait()
    build_filters(taps, lateral, depth)

    def channel(i):
        return 2 + core if i else 1 - core

    def foreign(c):
        return core == (0, 1, 1, 0)[c]

    def shot_copy(c, d, first, count):
        peer = lax.rem(s + d, shots)
        return pltpu.make_async_remote_copy(
            src_ref=images.at[peer, c, pl.ds(first, count)],
            dst_ref=gathered[c // 2].at[s, core, pl.ds(first, count)],
            send_sem=shot_send.at[c, d],
            recv_sem=shot_recv.at[c // 2, d, core],
            device_id=(peer, 2 * z + (1, 0, 0, 1)[c] if d else partner),
            device_id_type=MESH,
        )

    def shot_start(c, first, count):
        for d in range(1, shots):
            shot_copy(c, d, first, count).start()

        @pl.when(foreign(c))
        def _():
            shot_copy(c, 0, first, count).start()

    def shot_wait(i, d, a):
        return pltpu.make_async_remote_copy(
            src_ref=images.at[0, 0],
            dst_ref=gathered[i].at[lax.rem(s - d + shots, shots), a, pl.ds(0, panels)],
            send_sem=shot_send.at[0, d],
            recv_sem=shot_recv.at[i, d, a],
            device_id=(s, partner),
            device_id_type=MESH,
        )

    def parts(f, k, j):
        left = fields[f, k, 2 * j].reshape(192, NZ)
        right = fields[f, k, 2 * j + 1].reshape(192, NZ)
        both = jnp.concatenate([left, right], axis=1)
        flat = jnp.dot(lateral[...], both, preferred_element_type=jnp.float32)
        deep = jnp.dot(both, depth[...], preferred_element_type=jnp.float32)
        return (
            flat[0:64] + deep[128:192],
            flat[64:128] - deep[64:128],
            flat[128:192] + deep[0:64],
            flat[192:256],
        )

    @pl.loop(0, panels // BATCH)
    def _(q):
        first = q * BATCH
        for n in range(BATCH):
            k = first + n
            load(0, k).wait()
            load(1, k).wait()
            sums = None
            for j in range(levels // 2):
                a, a0, a1, a2 = parts(0, k, j)
                b, b0, b1, b2 = parts(1, k, j)
                new = (a * b, a * (b0 + b1 + b2), (a0 + a1 + a2) * b, a0 * b0 + a1 * b1 + a2 * b2)
                sums = new if sums is None else tuple(x + y for x, y in zip(sums, new))
            for c in range(4):
                image = (sums[c][:, :NZ] + sums[c][:, NZ:]).astype(jnp.bfloat16)
                images[:, c, k] = image.reshape(shots, width, NZ)

        @pl.when(q == 0)
        def _():
            pl.semaphore_wait(barrier, expected)

        shot_start(0, first, BATCH)

    for c in range(1, 4):
        shot_start(c, 0, panels)
    for i in range(2):
        gathered[i][s, core, 0:panels] = images[s, channel(i)]
        for g in range(shots):
            for a in range(2):
                gathered[i][g, a, panels] = jnp.zeros((width, NZ), jnp.bfloat16)

    near[1].wait()
    near[2].wait()
    slot_at = lax.broadcasted_iota(jnp.int32, (1, slots), 1)
    for g in range(shots):
        for a in range(2):
            found = jnp.full((1, slots), panels, jnp.int32)
            for k in range(panels):
                found = jnp.where(slot_at == tile_slot[aperture[g, (2 * z + a) * panels + k]], k, found)
            table_vector[2 * g + a : 2 * g + a + 1, :] = found
    table_copy = pltpu.make_async_copy(table_vector, table, table_sem)
    table_copy.start()

    near[3].wait()
    rows = pl.ds(pl.multiple_of(s * width, width), width)
    for r in range(owned):
        speed_p = model[r, 0, rows].astype(jnp.float32)
        speed_s = model[r, 1, rows].astype(jnp.float32)
        shear = model[r, 2, rows].astype(jnp.float32) * speed_s
        factor[0, r] = model[r, 2, rows].astype(jnp.float32) * speed_p
        factor[1, r] = shear
        factor[2, r] = shear * speed_s / speed_p
    table_copy.wait()

    def combined(i, row):
        total = None
        for g in range(shots):
            for a in range(2):
                term = gathered[i][g, a, table[2 * g + a, row]].astype(jnp.float32)
                total = term if total is None else total + term
        return total

    def relay_copy(i, block, o):
        return pltpu.make_async_remote_copy(
            src_ref=line_out.at[i, block, pl.ds(o * owned, owned)],
            dst_ref=relay_in.at[i, block, pl.ds(o * owned, owned)],
            send_sem=relay_send.at[i, block, o],
            recv_sem=relay_recv.at[i, block, o],
            device_id=(s, 2 * buddy + core),
            device_id_type=MESH,
        )

    def final_copy(i, block, o):
        c = channel(i)
        return pltpu.make_async_remote_copy(
            src_ref=line_out.at[i, block, pl.ds(o * owned, owned)],
            dst_ref=final_in.at[z // 2, c],
            send_sem=final_send.at[i, block, o],
            recv_sem=final_recv.at[z // 2, c],
            device_id=(s, 2 * block + o),
            device_id_type=MESH,
        )

    def final_wait(p, c):
        return pltpu.make_async_remote_copy(
            src_ref=line_out.at[0, 0, pl.ds(0, owned)],
            dst_ref=final_in.at[p, c],
            send_sem=final_send.at[0, 0, 0],
            recv_sem=final_recv.at[p, c],
            device_id=(s, partner),
            device_id_type=MESH,
        )

    def own_copy(i):
        return pltpu.make_async_remote_copy(
            src_ref=own_out.at[i],
            dst_ref=own_in.at[channel(i)],
            send_sem=own_send.at[i],
            recv_sem=own_recv.at[i],
            device_id=(s, partner),
            device_id_type=MESH,
        )

    def toward(block):
        return jnp.where(even, block > z, block < z)

    def arrived(i):
        for d in range(1, shots):
            for a in range(2):
                shot_wait(i, d, a).wait_recv()
        shot_wait(i, 0, 1 - core).wait_recv()

    def far(i):
        @pl.loop(0, chips)
        def _(j):
            block = jnp.where(even, chips - 1 - j, j)

            @pl.when(jnp.logical_and(toward(block), block != buddy))
            def _():
                for o in range(2):
                    for r in range(o * owned, (o + 1) * owned):
                        line_out[i, block, r] = combined(i, 2 * block * owned + r).astype(jnp.bfloat16)
                    relay_copy(i, block, o).start()

    def near_by(i):
        for o in range(2):
            for r in range(o * owned, (o + 1) * owned):
                line_out[i, buddy, r] = combined(i, 2 * buddy * owned + r).astype(jnp.bfloat16)
            final_copy(i, buddy, o).start()

    def here(i):
        for r in range(owned):
            own_out[i, r] = combined(i, (2 * z + 1 - core) * owned + r).astype(jnp.bfloat16)
        own_copy(i).start()
        for r in range(owned):
            own_in[channel(i), r] = combined(i, t * owned + r).astype(jnp.bfloat16)

    def relay(i):
        @pl.loop(0, chips)
        def _(j):
            block = jnp.where(even, j, chips - 1 - j)

            @pl.when(jnp.logical_and(block != z, jnp.logical_not(toward(block))))
            def _():
                for o in range(2):
                    relay_copy(i, block, o).wait_recv()
                    for r in range(o * owned, (o + 1) * owned):
                        total = combined(i, 2 * block * owned + r) + relay_in[i, block, r].astype(jnp.float32)
                        line_out[i, block, r] = total.astype(jnp.bfloat16)
                    final_copy(i, block, o).start()

    def finish(c):
        @pl.when(foreign(c))
        def _():
            own_copy(c // 2).wait_recv()

        for p in range(chips // 2):
            final_wait(p, c).wait_recv()
        for r in range(owned):
            total = own_in[c, r].astype(jnp.float32)
            for p in range(chips // 2):
                total = total + final_in[p, c, r].astype(jnp.float32)
            out[r, c] = factor[(0, 1, 1, 2)[c], r] * total

    arrived(0)
    far(0)

    @pl.when(core == 1)
    def _():
        near_by(0)

    here(0)
    relay(0)
    arrived(1)
    far(1)

    @pl.when(core == 0)
    def _():
        near_by(0)

    near_by(1)
    here(1)
    relay(1)
    for c in range(4):
        finish(c)

    for c in range(4):
        for d in range(1, shots):
            shot_copy(c, d, 0, panels).wait_send()

        @pl.when(foreign(c))
        def _():
            shot_copy(c, 0, 0, panels).wait_send()

    for i in range(2):
        own_copy(i).wait_send()

        @pl.loop(0, chips)
        def _(block):
            relayed = jnp.logical_and(toward(block), block != buddy)

            @pl.when(relayed)
            def _():
                relay_copy(i, block, 0).wait_send()
                relay_copy(i, block, 1).wait_send()

            @pl.when(jnp.logical_and(block != z, jnp.logical_not(relayed)))
            def _():
                final_copy(i, block, 0).wait_send()
                final_copy(i, block, 1).wait_send()


def tall(array):
    lead = array.shape[:-2]
    wide = array.shape[-1] // NZ
    array = array.reshape(lead + (8, wide, NZ))
    return jnp.swapaxes(array, -3, -2).reshape(lead + (8 * wide, NZ))


def body(src_field, rcv_field, model_panels, deriv_taps, aperture, tile_slot):
    tiles = lax.axis_size("tile")
    shots = lax.axis_size("shot")
    owned = model_panels.shape[0]
    panels, levels = src_field.shape[3], src_field.shape[1]
    chips = tiles // 2
    slots = tiles * owned
    width = 64 // shots

    vmem = pl.BlockSpec(memory_space=pltpu.VMEM)
    hbm = pl.BlockSpec(memory_space=pltpu.HBM)
    line = (2, chips, 2 * owned, width, NZ)
    result = pl.pallas_call(
        functools.partial(kernel, shots, tiles),
        out_shape=pltpu.VMEM((owned, 4, width, NZ), jnp.float32),
        in_specs=[hbm] * 6,
        out_specs=vmem,
        scratch_shapes=[
            pltpu.VMEM((2, panels, levels, 3, 64, NZ), jnp.bfloat16),
            pltpu.VMEM((256, 192), jnp.bfloat16),
            pltpu.VMEM((2 * NZ, 2 * NZ), jnp.bfloat16),
            pltpu.VMEM((shots, 4, panels, width, NZ), jnp.bfloat16),
            pltpu.VMEM((shots, 2, panels + 1, width, NZ), jnp.bfloat16),
            pltpu.VMEM((shots, 2, panels + 1, width, NZ), jnp.bfloat16),
            pltpu.VMEM(line, jnp.bfloat16),
            pltpu.VMEM(line, jnp.bfloat16),
            pltpu.VMEM((chips // 2, 4, owned, width, NZ), jnp.bfloat16),
            pltpu.VMEM((2, owned, width, NZ), jnp.bfloat16),
            pltpu.VMEM((4, owned, width, NZ), jnp.bfloat16),
            pltpu.SemaphoreType.DMA((2, panels)),
            pltpu.SemaphoreType.DMA((4, shots)),
            pltpu.SemaphoreType.DMA((2, shots, 2)),
            pltpu.SemaphoreType.DMA((2, chips, 2)),
            pltpu.SemaphoreType.DMA((2, chips, 2)),
            pltpu.SemaphoreType.DMA((2, chips, 2)),
            pltpu.SemaphoreType.DMA((chips // 2, 4)),
            pltpu.SemaphoreType.DMA((2,)),
            pltpu.SemaphoreType.DMA((2,)),
            pltpu.VMEM((2 * shots, slots), jnp.int32),
            pltpu.SMEM((2 * shots, slots), jnp.int32),
            pltpu.SemaphoreType.DMA,
            pltpu.SMEM(deriv_taps.shape, jnp.float32),
            pltpu.SMEM(aperture.shape, jnp.int32),
            pltpu.SMEM(tile_slot.shape, jnp.int32),
            pltpu.VMEM((owned, 3, 64, NZ), jnp.bfloat16),
            pltpu.SemaphoreType.DMA((4,)),
            pltpu.VMEM((3, owned, width, NZ), jnp.float32),
        ],
        compiler_params=pltpu.CompilerParams(collective_id=0, has_side_effects=True, vmem_limit_bytes=48 * 1024 * 1024),
    )(*[pltpu.with_memory_space_constraint(v, pltpu.HBM) for v in (deriv_taps, aperture, tile_slot, tall(src_field[0]), tall(rcv_field[0]), tall(model_panels))])

    def spill(near, far, sem):
        copies = [pltpu.make_async_copy(near.at[r], far.at[r], sem.at[r]) for r in range(owned)]
        for copy in copies:
            copy.start()
        for copy in copies:
            copy.wait()

    wide = jnp.swapaxes(result.reshape(owned, 4, width // 8, 8, NZ), 2, 3)
    return wide.reshape(owned, 4, 8, (width // 8) * NZ)


def solution(mesh):
    return jax.shard_map(
        body,
        mesh=mesh,
        in_specs=(
            P("shot", None, None, "tile", None, None),
            P("shot", None, None, "tile", None, None),
            P("tile", None, None, None),
            P(),
            P(),
            P(),
        ),
        out_specs=P("tile", None, None, "shot"),
        check_vma=False,
    )
```

```python
import functools

import jax
import jax.numpy as jnp
from jax import lax
from jax.experimental import pallas as pl
from jax.experimental.pallas import tpu as pltpu
from jax.sharding import PartitionSpec as P

MESH = pl.DeviceIdType.MESH
TAPS = 16
NZ = 128


def tap_values(taps, axis, offset):
    total = jnp.zeros(offset.shape, jnp.float32)
    for tap in range(TAPS):
        total = jnp.where(offset == tap, taps[axis, tap], total)
    return total


def build_filters(taps, lateral, depth):
    rows = lax.broadcasted_iota(jnp.int32, (32, 64), 0)
    cols = lax.broadcasted_iota(jnp.int32, (32, 64), 1)
    none = jnp.zeros((32, 64), jnp.float32)
    for half in range(2):
        at_y = 2 * (rows // 8) + half
        along_x = jnp.where(at_y == cols // 8, tap_values(taps, 0, cols % 8 - rows % 8 + 8), 0.0)
        along_y = jnp.where(rows % 8 == cols % 8, tap_values(taps, 1, cols // 8 - at_y + 8), 0.0)
        table = (
            (along_x, along_y, none),
            (none, none, along_y),
            (none, none, -along_x),
            (-along_y, along_x, none),
        )
        for out, line in enumerate(table):
            first = half * 128 + out * 32
            lateral[first : first + 32, :] = jnp.concatenate(line, axis=1).astype(jnp.bfloat16)
    rows = lax.broadcasted_iota(jnp.int32, (NZ, NZ), 0)
    cols = lax.broadcasted_iota(jnp.int32, (NZ, NZ), 1)
    along_z = tap_values(taps, 2, rows - cols + 8).astype(jnp.bfloat16)
    zeros = jnp.zeros((NZ, NZ), jnp.bfloat16)
    depth[:NZ, :NZ] = along_z
    depth[:NZ, NZ:] = zeros
    depth[NZ:, :NZ] = zeros
    depth[NZ:, NZ:] = along_z


def kernel(shots, tiles, taps_far, aperture_far, tile_slot_far, src, rcv, model_far, out, fields, lateral, depth, images, gathered_first, gathered_second,
           line_out, relay_in, final_in, own_out, own_in, load_sem, shot_send, shot_recv, relay_send, relay_recv,
           final_send, final_recv, own_send, own_recv, table_vector, table, table_sem,
           taps, aperture, tile_slot, model, near_sem, factor):
    s = lax.axis_index("shot")
    t = lax.axis_index("tile")
    chips = tiles // 2
    z, core = t // 2, t % 2
    even = z % 2 == 0
    buddy = z + 1 - 2 * (z % 2)
    partner = t + 1 - 2 * core
    panels, levels = fields.shape[1], fields.shape[2]
    owned = out.shape[0]
    slots = tiles * owned
    width = 64 // shots
    gathered = (gathered_first, gathered_second)

    def load(f, k):
        return pltpu.make_async_copy((src, rcv)[f].at[:, :, k], fields.at[f, k], load_sem.at[f, k])

    near = [
        pltpu.make_async_copy(far, ref, near_sem.at[i])
        for i, (far, ref) in enumerate(
            ((taps_far, taps), (aperture_far, aperture), (tile_slot_far, tile_slot), (model_far, model))
        )
    ]
    for copy in near[:3]:
        copy.start()

    @pl.loop(0, panels)
    def _(k):
        load(0, k).start()
        load(1, k).start()

    near[3].start()

    def meets(other):
        apart = jnp.where(other > z, jnp.logical_or(z % 2 == 1, other % 2 == 0), jnp.logical_or(even, other % 2 == 1))
        return jnp.logical_and(other != z, jnp.logical_or(other == buddy, apart))

    barrier = pltpu.get_barrier_semaphore()
    expected = 2 * (shots - 1) + 1
    for d in range(1, shots):
        for h in range(2):
            pl.semaphore_signal(barrier, inc=1, device_id=(lax.rem(s + d, shots), 2 * z + h), device_id_type=MESH)
    pl.semaphore_signal(barrier, inc=1, device_id=(s, partner), device_id_type=MESH)
    for other in range(chips):
        expected = expected + jnp.where(meets(other), 2, 0)

        @pl.when(meets(other))
        def _():
            for h in range(2):
                pl.semaphore_signal(barrier, inc=1, device_id=(s, 2 * other + h), device_id_type=MESH)

    near[0].wait()
    build_filters(taps, lateral, depth)
    near[1].wait()
    near[2].wait()
    slot_at = lax.broadcasted_iota(jnp.int32, (1, slots), 1)
    for g in range(shots):
        for a in range(2):
            found = jnp.full((1, slots), panels, jnp.int32)
            for k in range(panels):
                found = jnp.where(slot_at == tile_slot[aperture[g, (2 * z + a) * panels + k]], k, found)
            table_vector[2 * g + a : 2 * g + a + 1, :] = found
    table_copy = pltpu.make_async_copy(table_vector, table, table_sem)
    table_copy.start()
    for i in range(2):
        for g in range(shots):
            for a in range(2):
                gathered[i][g, a, panels] = jnp.zeros((width, NZ), jnp.bfloat16)

    def channel(i):
        return 2 + core if i else 1 - core

    def foreign(c):
        return core == (0, 1, 1, 0)[c]

    def shot_copy(c, d, first, count):
        peer = lax.rem(s + d, shots)
        return pltpu.make_async_remote_copy(
            src_ref=images.at[peer, c, pl.ds(first, count)],
            dst_ref=gathered[c // 2].at[s, core, pl.ds(first, count)],
            send_sem=shot_send.at[c, d],
            recv_sem=shot_recv.at[c // 2, d, core],
            device_id=(peer, 2 * z + (1, 0, 0, 1)[c] if d else partner),
            device_id_type=MESH,
        )

    def shot_start(c, first, count):
        for d in range(1, shots):
            shot_copy(c, d, first, count).start()

        @pl.when(foreign(c))
        def _():
            shot_copy(c, 0, first, count).start()

    def shot_wait(i, d, a):
        return pltpu.make_async_remote_copy(
            src_ref=images.at[0, 0],
            dst_ref=gathered[i].at[lax.rem(s - d + shots, shots), a, pl.ds(0, panels)],
            send_sem=shot_send.at[0, d],
            recv_sem=shot_recv.at[i, d, a],
            device_id=(s, partner),
            device_id_type=MESH,
        )

    def parts(f, k, j, half):
        left, right = fields[f, k, 2 * j], fields[f, k, 2 * j + 1]
        both = jnp.concatenate([left.reshape(192, NZ), right.reshape(192, NZ)], axis=1)
        wide = both.astype(jnp.float32)
        some = jnp.concatenate([wide[8 * y : 8 * y + 8] for y in range(half, 24, 2)], axis=0).astype(jnp.bfloat16)
        flat = jnp.dot(lateral[half * 128 : half * 128 + 128], both, preferred_element_type=jnp.float32)
        deep = jnp.dot(some, depth[...], preferred_element_type=jnp.float32)
        return flat[0:32] + deep[64:96], flat[32:64] - deep[32:64], flat[64:96] + deep[0:32], flat[96:128]

    for half in range(2):
        batch = (2, 4)[half]
        last = panels // batch - 1

        @pl.loop(0, panels // batch)
        def _(q):
            if half == 0:
                for n in range(batch):
                    load(0, q * batch + n).wait()
                    load(1, q * batch + n).wait()
            for n in range(batch):
                k = q * batch + n
                sums = None
                for j in range(levels // 2):
                    a, a0, a1, a2 = parts(0, k, j, half)
                    b, b0, b1, b2 = parts(1, k, j, half)
                    new = (a * b, a * (b0 + b1 + b2), (a0 + a1 + a2) * b, a0 * b0 + a1 * b1 + a2 * b2)
                    sums = new if sums is None else tuple(x + y for x, y in zip(sums, new))
                image = [(total[:, :NZ] + total[:, NZ:]).reshape(shots, 8, NZ) for total in sums]
                images[:, 3 * half, k] = jnp.concatenate(image[:2], axis=1).astype(jnp.bfloat16)
                images[:, 1 + half, k] = jnp.concatenate(image[2:], axis=1).astype(jnp.bfloat16)
            if half == 0:
                @pl.when(q == last - 1)
                def _():
                    pl.semaphore_wait(barrier, expected)
                    shot_start(0, 0, panels - batch)

                @pl.when(q == last)
                def _():
                    shot_start(0, panels - batch, batch)

        for c in range(1 + half, 2 + 2 * half):
            shot_start(c, 0, panels)
        gathered[half][s, core, 0:panels] = images[s, channel(half)]

    table_copy.wait()

    def combined(i, row):
        total = None
        for g in range(shots):
            for a in range(2):
                term = gathered[i][g, a, table[2 * g + a, row]].astype(jnp.float32)
                total = term if total is None else total + term
        return total

    def relay_copy(i, block, o):
        return pltpu.make_async_remote_copy(
            src_ref=line_out.at[i, block, pl.ds(o * owned, owned)],
            dst_ref=relay_in.at[i, block, pl.ds(o * owned, owned)],
            send_sem=relay_send.at[i, block, o],
            recv_sem=relay_recv.at[i, block, o],
            device_id=(s, 2 * buddy + core),
            device_id_type=MESH,
        )

    def final_copy(i, block, o):
        c = channel(i)
        return pltpu.make_async_remote_copy(
            src_ref=line_out.at[i, block, pl.ds(o * owned, owned)],
            dst_ref=final_in.at[z // 2, c],
            send_sem=final_send.at[i, block, o],
            recv_sem=final_recv.at[z // 2, c],
            device_id=(s, 2 * block + o),
            device_id_type=MESH,
        )

    def final_wait(p, c):
        return pltpu.make_async_remote_copy(
            src_ref=line_out.at[0, 0, pl.ds(0, owned)],
            dst_ref=final_in.at[p, c],
            send_sem=final_send.at[0, 0, 0],
            recv_sem=final_recv.at[p, c],
            device_id=(s, partner),
            device_id_type=MESH,
        )

    def own_copy(i):
        return pltpu.make_async_remote_copy(
            src_ref=own_out.at[i],
            dst_ref=own_in.at[channel(i)],
            send_sem=own_send.at[i],
            recv_sem=own_recv.at[i],
            device_id=(s, partner),
            device_id_type=MESH,
        )

    def toward(block):
        return jnp.where(even, block > z, block < z)

    def arrived(i):
        for d in range(1, shots):
            for a in range(2):
                shot_wait(i, d, a).wait_recv()
        shot_wait(i, 0, 1 - core).wait_recv()

    def far(i):
        @pl.loop(0, chips)
        def _(j):
            block = jnp.where(even, chips - 1 - j, j)

            @pl.when(jnp.logical_and(toward(block), block != buddy))
            def _():
                for o in range(2):
                    for r in range(o * owned, (o + 1) * owned):
                        line_out[i, block, r] = combined(i, 2 * block * owned + r).astype(jnp.bfloat16)
                    relay_copy(i, block, o).start()

    def near_by(i):
        for o in range(2):
            for r in range(o * owned, (o + 1) * owned):
                line_out[i, buddy, r] = combined(i, 2 * buddy * owned + r).astype(jnp.bfloat16)
            final_copy(i, buddy, o).start()

    def here(i):
        for r in range(owned):
            own_out[i, r] = combined(i, (2 * z + 1 - core) * owned + r).astype(jnp.bfloat16)
        own_copy(i).start()
        for r in range(owned):
            own_in[channel(i), r] = combined(i, t * owned + r).astype(jnp.bfloat16)

    def relay(i):
        @pl.loop(0, chips)
        def _(j):
            block = jnp.where(even, j, chips - 1 - j)

            @pl.when(jnp.logical_and(block != z, jnp.logical_not(toward(block))))
            def _():
                for o in range(2):
                    relay_copy(i, block, o).wait_recv()
                    for r in range(o * owned, (o + 1) * owned):
                        total = combined(i, 2 * block * owned + r) + relay_in[i, block, r].astype(jnp.float32)
                        line_out[i, block, r] = total.astype(jnp.bfloat16)
                    final_copy(i, block, o).start()

    def finish(c):
        @pl.when(foreign(c))
        def _():
            own_copy(c // 2).wait_recv()

        for p in range(chips // 2):
            final_wait(p, c).wait_recv()
        for r in range(owned):
            total = own_in[c, r].astype(jnp.float32)
            for p in range(chips // 2):
                total = total + final_in[p, c, r].astype(jnp.float32)
            near_y = slice(c // 2 * 8, c // 2 * 8 + 8)
            for kind in range(2):
                image = kind if c in (0, 3) else kind + 2
                out[r, image, near_y] = factor[(0, 1, 1, 2)[image], r, near_y] * total[kind * 8 : kind * 8 + 8]

    arrived(0)
    far(0)

    @pl.when(core == 1)
    def _():
        near_by(0)

    here(0)
    relay(0)
    near[3].wait()
    rows = pl.ds(pl.multiple_of(s * width, width), width)
    for r in range(owned):
        speed_p = model[r, 0, rows].astype(jnp.float32)
        speed_s = model[r, 1, rows].astype(jnp.float32)
        shear = model[r, 2, rows].astype(jnp.float32) * speed_s
        factor[0, r] = model[r, 2, rows].astype(jnp.float32) * speed_p
        factor[1, r] = shear
        factor[2, r] = shear * speed_s / speed_p
    arrived(1)
    far(1)

    @pl.when(core == 0)
    def _():
        near_by(0)

    near_by(1)
    here(1)
    relay(1)
    for c in range(4):
        finish(c)

    for c in range(4):
        for d in range(1, shots):
            shot_copy(c, d, 0, panels).wait_send()

        @pl.when(foreign(c))
        def _():
            shot_copy(c, 0, 0, panels).wait_send()

    for i in range(2):
        own_copy(i).wait_send()

        @pl.loop(0, chips)
        def _(block):
            relayed = jnp.logical_and(toward(block), block != buddy)

            @pl.when(relayed)
            def _():
                relay_copy(i, block, 0).wait_send()
                relay_copy(i, block, 1).wait_send()

            @pl.when(jnp.logical_and(block != z, jnp.logical_not(relayed)))
            def _():
                final_copy(i, block, 0).wait_send()
                final_copy(i, block, 1).wait_send()


def tall(array):
    lead = array.shape[:-2]
    wide = array.shape[-1] // NZ
    array = array.reshape(lead + (8, wide, NZ))
    return jnp.swapaxes(array, -3, -2).reshape(lead + (8 * wide, NZ))


def body(src_field, rcv_field, model_panels, deriv_taps, aperture, tile_slot):
    tiles = lax.axis_size("tile")
    shots = lax.axis_size("shot")
    owned = model_panels.shape[0]
    panels, levels = src_field.shape[3], src_field.shape[1]
    chips = tiles // 2
    slots = tiles * owned
    width = 64 // shots

    vmem = pl.BlockSpec(memory_space=pltpu.VMEM)
    hbm = pl.BlockSpec(memory_space=pltpu.HBM)
    line = (2, chips, 2 * owned, width, NZ)
    result = pl.pallas_call(
        functools.partial(kernel, shots, tiles),
        out_shape=pltpu.VMEM((owned, 4, width, NZ), jnp.float32),
        in_specs=[hbm] * 6,
        out_specs=vmem,
        scratch_shapes=[
            pltpu.VMEM((2, panels, levels, 3, 64, NZ), jnp.bfloat16),
            pltpu.VMEM((256, 192), jnp.bfloat16),
            pltpu.VMEM((2 * NZ, 2 * NZ), jnp.bfloat16),
            pltpu.VMEM((shots, 4, panels, width, NZ), jnp.bfloat16),
            pltpu.VMEM((shots, 2, panels + 1, width, NZ), jnp.bfloat16),
            pltpu.VMEM((shots, 2, panels + 1, width, NZ), jnp.bfloat16),
            pltpu.VMEM(line, jnp.bfloat16),
            pltpu.VMEM(line, jnp.bfloat16),
            pltpu.VMEM((chips // 2, 4, owned, width, NZ), jnp.bfloat16),
            pltpu.VMEM((2, owned, width, NZ), jnp.bfloat16),
            pltpu.VMEM((4, owned, width, NZ), jnp.bfloat16),
            pltpu.SemaphoreType.DMA((2, panels)),
            pltpu.SemaphoreType.DMA((4, shots)),
            pltpu.SemaphoreType.DMA((2, shots, 2)),
            pltpu.SemaphoreType.DMA((2, chips, 2)),
            pltpu.SemaphoreType.DMA((2, chips, 2)),
            pltpu.SemaphoreType.DMA((2, chips, 2)),
            pltpu.SemaphoreType.DMA((chips // 2, 4)),
            pltpu.SemaphoreType.DMA((2,)),
            pltpu.SemaphoreType.DMA((2,)),
            pltpu.VMEM((2 * shots, slots), jnp.int32),
            pltpu.SMEM((2 * shots, slots), jnp.int32),
            pltpu.SemaphoreType.DMA,
            pltpu.SMEM(deriv_taps.shape, jnp.float32),
            pltpu.SMEM(aperture.shape, jnp.int32),
            pltpu.SMEM(tile_slot.shape, jnp.int32),
            pltpu.VMEM((owned, 3, 64, NZ), jnp.bfloat16),
            pltpu.SemaphoreType.DMA((4,)),
            pltpu.VMEM((3, owned, width, NZ), jnp.float32),
        ],
        compiler_params=pltpu.CompilerParams(collective_id=0, has_side_effects=True, vmem_limit_bytes=48 * 1024 * 1024),
    )(*[pltpu.with_memory_space_constraint(v, pltpu.HBM) for v in (deriv_taps, aperture, tile_slot, tall(src_field[0]), tall(rcv_field[0]), tall(model_panels))])

    def spill(near, far, sem):
        copies = [pltpu.make_async_copy(near.at[r], far.at[r], sem.at[r]) for r in range(owned)]
        for copy in copies:
            copy.start()
        for copy in copies:
            copy.wait()

    wide = jnp.swapaxes(result.reshape(owned, 4, width // 8, 8, NZ), 2, 3)
    return wide.reshape(owned, 4, 8, (width // 8) * NZ)


def solution(mesh):
    return jax.shard_map(
        body,
        mesh=mesh,
        in_specs=(
            P("shot", None, None, "tile", None, None),
            P("shot", None, None, "tile", None, None),
            P("tile", None, None, None),
            P(),
            P(),
            P(),
        ),
        out_specs=P("tile", None, None, "shot"),
        check_vma=False,
    )
```

```python
import functools

import jax
import jax.numpy as jnp
from jax import lax
from jax.experimental import pallas as pl
from jax.experimental.pallas import tpu as pltpu
from jax.sharding import PartitionSpec as P

MESH = pl.DeviceIdType.MESH
TAPS = 16
NZ = 128


def tap_values(taps, axis, offset):
    total = jnp.zeros(offset.shape, jnp.float32)
    for tap in range(TAPS):
        total = jnp.where(offset == tap, taps[axis, tap], total)
    return total


def build_filters(taps, lateral, depth):
    rows = lax.broadcasted_iota(jnp.int32, (32, 64), 0)
    cols = lax.broadcasted_iota(jnp.int32, (32, 64), 1)
    none = jnp.zeros((32, 64), jnp.float32)
    for half in range(2):
        at_y = 2 * (rows // 8) + half
        along_x = jnp.where(at_y == cols // 8, tap_values(taps, 0, cols % 8 - rows % 8 + 8), 0.0)
        along_y = jnp.where(rows % 8 == cols % 8, tap_values(taps, 1, cols // 8 - at_y + 8), 0.0)
        table = (
            (along_x, along_y, none),
            (none, none, along_y),
            (none, none, -along_x),
            (-along_y, along_x, none),
        )
        for out, line in enumerate(table):
            first = half * 128 + out * 32
            lateral[first : first + 32, :] = jnp.concatenate(line, axis=1).astype(jnp.bfloat16)
    rows = lax.broadcasted_iota(jnp.int32, (NZ, NZ), 0)
    cols = lax.broadcasted_iota(jnp.int32, (NZ, NZ), 1)
    along_z = tap_values(taps, 2, rows - cols + 8).astype(jnp.bfloat16)
    zeros = jnp.zeros((NZ, NZ), jnp.bfloat16)
    depth[:NZ, :NZ] = along_z
    depth[:NZ, NZ:] = zeros
    depth[NZ:, :NZ] = zeros
    depth[NZ:, NZ:] = along_z


def kernel(shots, tiles, taps_far, aperture_far, tile_slot_far, src, rcv, model_far, out, fields, lateral, depth, images, gathered, gathered_pair,
           line_out, line_pair, relay_in, final_in, own_out, own_in, load_sem, shot_send, shot_recv, pair_recv, relay_send, relay_recv,
           final_send, pair_send, final_recv, own_send, own_recv, table_vector, table, table_sem, pair_vector, pair_table,
           taps, aperture, tile_slot, model, near_sem, factor):
    s = lax.axis_index("shot")
    t = lax.axis_index("tile")
    chips = tiles // 2
    z, core = t // 2, t % 2
    even = z % 2 == 0
    buddy = z + 1 - 2 * (z % 2)
    partner = t + 1 - 2 * core
    panels, levels = fields.shape[1], fields.shape[2]
    owned = out.shape[0]
    slots = tiles * owned
    width = 64 // shots
    dense, paired = 2 - 2 * core, 1 + 2 * core
    pair, side = z // 2, z % 2

    def hub_of(chip):
        return chip // 2 * 2 + jnp.where(chip // 2 < chips // 4, 1, 0)

    hub = hub_of(z)
    is_hub = z == hub

    def load(f, k):
        return pltpu.make_async_copy((src, rcv)[f].at[:, :, k], fields.at[f, k], load_sem.at[f, k])

    near = [
        pltpu.make_async_copy(far, ref, near_sem.at[i])
        for i, (far, ref) in enumerate(
            ((taps_far, taps), (aperture_far, aperture), (tile_slot_far, tile_slot), (model_far, model))
        )
    ]
    for copy in near[:3]:
        copy.start()

    @pl.loop(0, panels)
    def _(k):
        load(0, k).start()
        load(1, k).start()

    near[3].start()

    def meets(other):
        apart = jnp.where(other > z, jnp.logical_or(z % 2 == 1, other % 2 == 0), jnp.logical_or(even, other % 2 == 1))
        direct = jnp.logical_or(apart, jnp.logical_or(is_hub, hub_of(other) == other))
        return jnp.logical_and(other != z, jnp.logical_or(other == buddy, direct))

    barrier = pltpu.get_barrier_semaphore()
    expected = 2 * (shots - 1) + 1 + jnp.where(is_hub, 0, 2 * (shots - 1))
    for d in range(1, shots):
        for h in range(2):
            pl.semaphore_signal(barrier, inc=1, device_id=(lax.rem(s + d, shots), 2 * z + h), device_id_type=MESH)
    pl.semaphore_signal(barrier, inc=1, device_id=(s, partner), device_id_type=MESH)
    for other in range(chips):
        expected = expected + jnp.where(meets(other), 2, 0)

        @pl.when(meets(other))
        def _():
            for h in range(2):
                pl.semaphore_signal(barrier, inc=1, device_id=(s, 2 * other + h), device_id_type=MESH)

    @pl.when(is_hub)
    def _():
        for d in range(1, shots):
            for h in range(2):
                pl.semaphore_signal(
                    barrier, inc=1, device_id=(lax.rem(s + d, shots), 2 * buddy + h), device_id_type=MESH
                )

    near[0].wait()
    build_filters(taps, lateral, depth)
    near[1].wait()
    near[2].wait()
    slot_at = lax.broadcasted_iota(jnp.int32, (1, slots), 1)
    for g in range(shots):
        for a in range(2):
            found = jnp.full((1, slots), panels, jnp.int32)
            for k in range(panels):
                found = jnp.where(slot_at == tile_slot[aperture[g, (2 * z + a) * panels + k]], k, found)
            table_vector[2 * g + a : 2 * g + a + 1, :] = found
    table_copy = pltpu.make_async_copy(table_vector, table, table_sem)
    table_copy.start()
    for g in range(shots):
        for a in range(2):
            gathered[g, a, panels] = jnp.zeros((width, NZ), jnp.bfloat16)
            for n in range(2):
                gathered_pair[n, g, a, panels] = jnp.zeros((width, NZ), jnp.bfloat16)
    for c in (1, 3):
        @pl.when(is_hub)
        def _():
            final_in[pair, c] = jnp.zeros((owned, width, NZ), jnp.bfloat16)

        @pl.when(jnp.logical_not(is_hub))
        def _():
            own_in[c] = jnp.zeros((owned, width, NZ), jnp.bfloat16)

    def foreign(c):
        return core == (0, 1, 1, 0)[c]

    def shot_copy(c, d, first, count):
        peer = lax.rem(s + d, shots)
        return pltpu.make_async_remote_copy(
            src_ref=images.at[peer, c, pl.ds(first, count)],
            dst_ref=gathered.at[s, core, pl.ds(first, count)],
            send_sem=shot_send.at[c, d],
            recv_sem=shot_recv.at[d, core],
            device_id=(peer, 2 * z + (1, 0, 0, 1)[c] if d else partner),
            device_id_type=MESH,
        )

    def shot_start(c, first, count):
        for d in range(1, shots):
            shot_copy(c, d, first, count).start()

        @pl.when(foreign(c))
        def _():
            shot_copy(c, 0, first, count).start()

    def pair_copy(c, d):
        peer = lax.rem(s + d, shots)
        return pltpu.make_async_remote_copy(
            src_ref=images.at[peer, c],
            dst_ref=gathered_pair.at[side, s, core, pl.ds(0, panels)],
            send_sem=shot_send.at[c, d],
            recv_sem=pair_recv.at[d, side, core],
            device_id=(peer, 2 * hub + (0, 0, 1, 1)[c]),
            device_id_type=MESH,
        )

    def pair_leaves(c):
        return jnp.logical_or(jnp.logical_not(is_hub), foreign(c))

    def pair_start(c):
        @pl.when(pair_leaves(c))
        def _():
            pair_copy(c, 0).start()

        for d in range(1, shots):
            pair_copy(c, d).start()

    def pair_wait(d, from_side, a):
        return pltpu.make_async_remote_copy(
            src_ref=images.at[0, 0],
            dst_ref=gathered_pair.at[from_side, lax.rem(s - d + shots, shots), a, pl.ds(0, panels)],
            send_sem=shot_send.at[1, d],
            recv_sem=pair_recv.at[d, from_side, a],
            device_id=(s, partner),
            device_id_type=MESH,
        )

    def shot_wait(d, a):
        return pltpu.make_async_remote_copy(
            src_ref=images.at[0, 0],
            dst_ref=gathered.at[lax.rem(s - d + shots, shots), a, pl.ds(0, panels)],
            send_sem=shot_send.at[0, d],
            recv_sem=shot_recv.at[d, a],
            device_id=(s, partner),
            device_id_type=MESH,
        )

    def parts(f, k, j, half):
        left, right = fields[f, k, 2 * j], fields[f, k, 2 * j + 1]
        both = jnp.concatenate([left.reshape(192, NZ), right.reshape(192, NZ)], axis=1)
        wide = both.astype(jnp.float32)
        some = jnp.concatenate([wide[8 * y : 8 * y + 8] for y in range(half, 24, 2)], axis=0).astype(jnp.bfloat16)
        flat = jnp.dot(lateral[half * 128 : half * 128 + 128], both, preferred_element_type=jnp.float32)
        deep = jnp.dot(some, depth[...], preferred_element_type=jnp.float32)
        return flat[0:32] + deep[64:96], flat[32:64] - deep[32:64], flat[64:96] + deep[0:32], flat[96:128]

    for half in range(2):
        batch = (2, 4)[half]
        last = panels // batch - 1

        @pl.loop(0, panels // batch)
        def _(q):
            if half == 0:
                for n in range(batch):
                    load(0, q * batch + n).wait()
                    load(1, q * batch + n).wait()
            for n in range(batch):
                k = q * batch + n
                sums = None
                for j in range(levels // 2):
                    a, a0, a1, a2 = parts(0, k, j, half)
                    b, b0, b1, b2 = parts(1, k, j, half)
                    new = (a * b, a * (b0 + b1 + b2), (a0 + a1 + a2) * b, a0 * b0 + a1 * b1 + a2 * b2)
                    sums = new if sums is None else tuple(x + y for x, y in zip(sums, new))
                image = [(total[:, :NZ] + total[:, NZ:]).reshape(shots, 8, NZ) for total in sums]
                images[:, 3 * half, k] = jnp.concatenate(image[:2], axis=1).astype(jnp.bfloat16)
                images[:, 1 + half, k] = jnp.concatenate(image[2:], axis=1).astype(jnp.bfloat16)
            if half == 0:
                @pl.when(q == last - 1)
                def _():
                    pl.semaphore_wait(barrier, expected)
                    shot_start(0, 0, panels - batch)

                @pl.when(q == last)
                def _():
                    shot_start(0, panels - batch, batch)

        if half == 0:
            pair_start(1)
        else:
            shot_start(2, 0, panels)
            pair_start(3)

    gathered[s, core, 0:panels] = images[s, dense]
    table_copy.wait()

    @pl.when(is_hub)
    def _():
        gathered_pair[side, s, core, 0:panels] = images[s, paired]
        for n in range(2):
            for g in range(shots):
                for a in range(2):
                    found = jnp.full((1, slots), panels, jnp.int32)
                    for k in range(panels):
                        place = (2 * (2 * pair + n) + a) * panels + k
                        found = jnp.where(slot_at == tile_slot[aperture[g, place]], k, found)
                    line = (n * shots + g) * 2 + a
                    pair_vector[line : line + 1, :] = found
        whole = pltpu.make_async_copy(pair_vector, pair_table, table_sem)
        whole.start()
        whole.wait()

    def combined(row):
        total = None
        for g in range(shots):
            for a in range(2):
                term = gathered[g, a, table[2 * g + a, row]].astype(jnp.float32)
                total = term if total is None else total + term
        return total

    def pair_combined(row):
        total = None
        for n in range(2):
            for g in range(shots):
                for a in range(2):
                    at = pair_table[(n * shots + g) * 2 + a, row]
                    term = gathered_pair[n, g, a, at].astype(jnp.float32)
                    total = term if total is None else total + term
        return total

    def pair_final(block, o):
        return pltpu.make_async_remote_copy(
            src_ref=line_pair.at[block, pl.ds(o * owned, owned)],
            dst_ref=final_in.at[pair, paired],
            send_sem=pair_send.at[block, o],
            recv_sem=final_recv.at[pair, paired],
            device_id=(s, 2 * block + o),
            device_id_type=MESH,
        )

    def relay_copy(block, o):
        return pltpu.make_async_remote_copy(
            src_ref=line_out.at[block, pl.ds(o * owned, owned)],
            dst_ref=relay_in.at[block, pl.ds(o * owned, owned)],
            send_sem=relay_send.at[block, o],
            recv_sem=relay_recv.at[block, o],
            device_id=(s, 2 * buddy + core),
            device_id_type=MESH,
        )

    def final_copy(block, o):
        return pltpu.make_async_remote_copy(
            src_ref=line_out.at[block, pl.ds(o * owned, owned)],
            dst_ref=final_in.at[pair, dense],
            send_sem=final_send.at[block, o],
            recv_sem=final_recv.at[pair, dense],
            device_id=(s, 2 * block + o),
            device_id_type=MESH,
        )

    def final_wait(p, c):
        return pltpu.make_async_remote_copy(
            src_ref=line_out.at[0, pl.ds(0, owned)],
            dst_ref=final_in.at[p, c],
            send_sem=final_send.at[0, 0],
            recv_sem=final_recv.at[p, c],
            device_id=(s, partner),
            device_id_type=MESH,
        )

    def own_copy(kind):
        return pltpu.make_async_remote_copy(
            src_ref=own_out.at[kind],
            dst_ref=own_in.at[paired if kind else dense],
            send_sem=own_send.at[kind],
            recv_sem=own_recv.at[kind],
            device_id=(s, partner),
            device_id_type=MESH,
        )

    def toward(block):
        return jnp.where(even, block > z, block < z)

    def rows_of(block, o):
        return [(o * owned + r, (2 * block + o) * owned + r) for r in range(owned)]

    def spread_dense():
        for d in range(1, shots):
            for a in range(2):
                shot_wait(d, a).wait_recv()
        shot_wait(0, 1 - core).wait_recv()

        @pl.loop(0, chips)
        def _(j):
            block = jnp.where(even, chips - 1 - j, j)

            @pl.when(toward(block))
            def _():
                for o in range(2):
                    for place, row in rows_of(block, o):
                        line_out[block, place] = combined(row).astype(jnp.bfloat16)

                    @pl.when(block == buddy)
                    def _():
                        final_copy(block, o).start()

                    @pl.when(block != buddy)
                    def _():
                        relay_copy(block, o).start()

        for r in range(owned):
            own_out[0, r] = combined((2 * z + 1 - core) * owned + r).astype(jnp.bfloat16)
        own_copy(0).start()
        for r in range(owned):
            own_in[dense, r] = combined(t * owned + r).astype(jnp.bfloat16)

        @pl.loop(0, chips)
        def _(j):
            block = jnp.where(even, j, chips - 1 - j)

            @pl.when(jnp.logical_and(block != z, jnp.logical_not(toward(block))))
            def _():
                for o in range(2):
                    relay_copy(block, o).wait_recv()
                    for place, row in rows_of(block, o):
                        total = combined(row) + relay_in[block, place].astype(jnp.float32)
                        line_out[block, place] = total.astype(jnp.bfloat16)
                    final_copy(block, o).start()

    def spread_pair():
        for d in range(1, shots):
            for a in range(2):
                pair_wait(d, 0, a).wait_recv()
                pair_wait(d, 1, a).wait_recv()
        pair_wait(0, side, 1 - core).wait_recv()
        pair_wait(0, 1 - side, 0).wait_recv()
        pair_wait(0, 1 - side, 1).wait_recv()

        @pl.loop(0, chips)
        def _(j):
            block = jnp.where(even, j, chips - 1 - j)

            @pl.when(block != z)
            def _():
                for o in range(2):
                    for place, row in rows_of(block, o):
                        line_pair[block, place] = pair_combined(row).astype(jnp.bfloat16)
                    pair_final(block, o).start()

        for r in range(owned):
            own_out[1, r] = pair_combined((2 * z + 1 - core) * owned + r).astype(jnp.bfloat16)
        own_copy(1).start()
        for r in range(owned):
            own_in[paired, r] = pair_combined(t * owned + r).astype(jnp.bfloat16)

    def finish(c):
        hubs = c % 2 == 1

        @pl.when(jnp.logical_and(foreign(c), is_hub) if hubs else foreign(c))
        def _():
            own_copy(c % 2).wait_recv()

        for p in range(chips // 2):
            if hubs:
                @pl.when(jnp.logical_or(p != pair, jnp.logical_not(is_hub)))
                def _():
                    final_wait(p, c).wait_recv()
            else:
                final_wait(p, c).wait_recv()
        for r in range(owned):
            total = own_in[c, r].astype(jnp.float32)
            for p in range(chips // 2):
                total = total + final_in[p, c, r].astype(jnp.float32)
            near_y = slice(c // 2 * 8, c // 2 * 8 + 8)
            for kind in range(2):
                image = kind if c in (0, 3) else kind + 2
                out[r, image, near_y] = factor[(0, 1, 1, 2)[image], r, near_y] * total[kind * 8 : kind * 8 + 8]

    near[3].wait()
    rows = pl.ds(pl.multiple_of(s * width, width), width)
    for r in range(owned):
        speed_p = model[r, 0, rows].astype(jnp.float32)
        speed_s = model[r, 1, rows].astype(jnp.float32)
        shear = model[r, 2, rows].astype(jnp.float32) * speed_s
        factor[0, r] = model[r, 2, rows].astype(jnp.float32) * speed_p
        factor[1, r] = shear
        factor[2, r] = shear * speed_s / speed_p
    @pl.loop(0, 2)
    def _(turn):
        pl.when(turn != core)(spread_dense)
        pl.when(jnp.logical_and(turn == core, is_hub))(spread_pair)

    for c in range(4):
        finish(c)

    for c in (0, 2):
        for d in range(1, shots):
            shot_copy(c, d, 0, panels).wait_send()

        @pl.when(foreign(c))
        def _():
            shot_copy(c, 0, 0, panels).wait_send()

    for c in (1, 3):
        for d in range(1, shots):
            pair_copy(c, d).wait_send()

        @pl.when(pair_leaves(c))
        def _():
            pair_copy(c, 0).wait_send()

    own_copy(0).wait_send()

    @pl.when(is_hub)
    def _():
        own_copy(1).wait_send()

    @pl.loop(0, chips)
    def _(block):
        relayed = jnp.logical_and(toward(block), block != buddy)
        for o in range(2):
            @pl.when(relayed)
            def _():
                relay_copy(block, o).wait_send()

            @pl.when(jnp.logical_and(block != z, jnp.logical_not(relayed)))
            def _():
                final_copy(block, o).wait_send()

            @pl.when(jnp.logical_and(block != z, is_hub))
            def _():
                pair_final(block, o).wait_send()


def tall(array):
    lead = array.shape[:-2]
    wide = array.shape[-1] // NZ
    array = array.reshape(lead + (8, wide, NZ))
    return jnp.swapaxes(array, -3, -2).reshape(lead + (8 * wide, NZ))


def body(src_field, rcv_field, model_panels, deriv_taps, aperture, tile_slot):
    tiles = lax.axis_size("tile")
    shots = lax.axis_size("shot")
    owned = model_panels.shape[0]
    panels, levels = src_field.shape[3], src_field.shape[1]
    chips = tiles // 2
    slots = tiles * owned
    width = 64 // shots

    vmem = pl.BlockSpec(memory_space=pltpu.VMEM)
    hbm = pl.BlockSpec(memory_space=pltpu.HBM)
    line = (chips, 2 * owned, width, NZ)
    result = pl.pallas_call(
        functools.partial(kernel, shots, tiles),
        out_shape=pltpu.VMEM((owned, 4, width, NZ), jnp.float32),
        in_specs=[hbm] * 6,
        out_specs=vmem,
        scratch_shapes=[
            pltpu.VMEM((2, panels, levels, 3, 64, NZ), jnp.bfloat16),
            pltpu.VMEM((256, 192), jnp.bfloat16),
            pltpu.VMEM((2 * NZ, 2 * NZ), jnp.bfloat16),
            pltpu.VMEM((shots, 4, panels, width, NZ), jnp.bfloat16),
            pltpu.VMEM((shots, 2, panels + 1, width, NZ), jnp.bfloat16),
            pltpu.VMEM((2, shots, 2, panels + 1, width, NZ), jnp.bfloat16),
            pltpu.VMEM(line, jnp.bfloat16),
            pltpu.VMEM(line, jnp.bfloat16),
            pltpu.VMEM(line, jnp.bfloat16),
            pltpu.VMEM((chips // 2, 4, owned, width, NZ), jnp.bfloat16),
            pltpu.VMEM((2, owned, width, NZ), jnp.bfloat16),
            pltpu.VMEM((4, owned, width, NZ), jnp.bfloat16),
            pltpu.SemaphoreType.DMA((2, panels)),
            pltpu.SemaphoreType.DMA((4, shots)),
            pltpu.SemaphoreType.DMA((shots, 2)),
            pltpu.SemaphoreType.DMA((shots, 2, 2)),
            pltpu.SemaphoreType.DMA((chips, 2)),
            pltpu.SemaphoreType.DMA((chips, 2)),
            pltpu.SemaphoreType.DMA((chips, 2)),
            pltpu.SemaphoreType.DMA((chips, 2)),
            pltpu.SemaphoreType.DMA((chips // 2, 4)),
            pltpu.SemaphoreType.DMA((2,)),
            pltpu.SemaphoreType.DMA((2,)),
            pltpu.VMEM((2 * shots, slots), jnp.int32),
            pltpu.SMEM((2 * shots, slots), jnp.int32),
            pltpu.SemaphoreType.DMA,
            pltpu.VMEM((4 * shots, slots), jnp.int32),
            pltpu.SMEM((4 * shots, slots), jnp.int32),
            pltpu.SMEM(deriv_taps.shape, jnp.float32),
            pltpu.SMEM(aperture.shape, jnp.int32),
            pltpu.SMEM(tile_slot.shape, jnp.int32),
            pltpu.VMEM((owned, 3, 64, NZ), jnp.bfloat16),
            pltpu.SemaphoreType.DMA((4,)),
            pltpu.VMEM((3, owned, width, NZ), jnp.float32),
        ],
        compiler_params=pltpu.CompilerParams(collective_id=0, has_side_effects=True, vmem_limit_bytes=48 * 1024 * 1024),
    )(*[pltpu.with_memory_space_constraint(v, pltpu.HBM) for v in (deriv_taps, aperture, tile_slot, tall(src_field[0]), tall(rcv_field[0]), tall(model_panels))])

    def spill(near, far, sem):
        copies = [pltpu.make_async_copy(near.at[r], far.at[r], sem.at[r]) for r in range(owned)]
        for copy in copies:
            copy.start()
        for copy in copies:
            copy.wait()

    wide = jnp.swapaxes(result.reshape(owned, 4, width // 8, 8, NZ), 2, 3)
    return wide.reshape(owned, 4, 8, (width // 8) * NZ)


def solution(mesh):
    return jax.shard_map(
        body,
        mesh=mesh,
        in_specs=(
            P("shot", None, None, "tile", None, None),
            P("shot", None, None, "tile", None, None),
            P("tile", None, None, None),
            P(),
            P(),
            P(),
        ),
        out_specs=P("tile", None, None, "shot"),
        check_vma=False,
    )
```

```python
import functools

import jax
import jax.numpy as jnp
from jax import lax
from jax.experimental import pallas as pl
from jax.experimental.pallas import tpu as pltpu
from jax.sharding import PartitionSpec as P

MESH = pl.DeviceIdType.MESH
TAPS = 16
NZ = 128


def tap_values(taps, axis, offset):
    total = jnp.zeros(offset.shape, jnp.float32)
    for tap in range(TAPS):
        total = jnp.where(offset == tap, taps[axis, tap], total)
    return total


def build_filters(taps, lateral, depth):
    rows = lax.broadcasted_iota(jnp.int32, (32, 64), 0)
    cols = lax.broadcasted_iota(jnp.int32, (32, 64), 1)
    none = jnp.zeros((32, 64), jnp.float32)
    for half in range(2):
        at_y = 2 * (rows // 8) + half
        along_x = jnp.where(at_y == cols // 8, tap_values(taps, 0, cols % 8 - rows % 8 + 8), 0.0)
        along_y = jnp.where(rows % 8 == cols % 8, tap_values(taps, 1, cols // 8 - at_y + 8), 0.0)
        table = (
            (along_x, along_y, none),
            (none, none, along_y),
            (none, none, -along_x),
            (-along_y, along_x, none),
        )
        for out, line in enumerate(table):
            first = half * 128 + out * 32
            lateral[first : first + 32, :] = jnp.concatenate(line, axis=1).astype(jnp.bfloat16)
    rows = lax.broadcasted_iota(jnp.int32, (NZ, NZ), 0)
    cols = lax.broadcasted_iota(jnp.int32, (NZ, NZ), 1)
    along_z = tap_values(taps, 2, rows - cols + 8).astype(jnp.bfloat16)
    zeros = jnp.zeros((NZ, NZ), jnp.bfloat16)
    depth[:NZ, :NZ] = along_z
    depth[:NZ, NZ:] = zeros
    depth[NZ:, :NZ] = zeros
    depth[NZ:, NZ:] = along_z


def kernel(shots, tiles, taps_far, aperture_far, tile_slot_far, src, rcv, model_far, out, fields, lateral, depth, images, gathered_first, gathered_second, gathered_pair,
           line_out, line_pair, relay_in, final_in, own_out, own_in, load_sem, shot_send, shot_recv, pair_recv, relay_send, relay_recv,
           final_send, pair_send, final_recv, own_send, own_recv, table_vector, table, table_sem, pair_vector, pair_table,
           taps, aperture, tile_slot, model, near_sem, factor):
    s = lax.axis_index("shot")
    t = lax.axis_index("tile")
    chips = tiles // 2
    z, core = t // 2, t % 2
    even = z % 2 == 0
    buddy = z + 1 - 2 * (z % 2)
    partner = t + 1 - 2 * core
    panels, levels = fields.shape[1], fields.shape[2]
    owned = out.shape[0]
    slots = tiles * owned
    width = 64 // shots
    gathered = (gathered_first, gathered_second)
    pair, side = z // 2, z % 2

    def hub_of(chip):
        return chip // 2 * 2 + jnp.where(chip // 2 < chips // 4, 1, 0)

    hub = hub_of(z)
    is_hub = z == hub
    gathers = jnp.logical_and(is_hub, core == 0)

    def load(f, k):
        return pltpu.make_async_copy((src, rcv)[f].at[:, :, k], fields.at[f, k], load_sem.at[f, k])

    near = [
        pltpu.make_async_copy(far, ref, near_sem.at[i])
        for i, (far, ref) in enumerate(
            ((taps_far, taps), (aperture_far, aperture), (tile_slot_far, tile_slot), (model_far, model))
        )
    ]
    for copy in near[:3]:
        copy.start()

    @pl.loop(0, panels)
    def _(k):
        load(0, k).start()
        load(1, k).start()

    near[3].start()

    def meets(other):
        apart = jnp.where(other > z, jnp.logical_or(z % 2 == 1, other % 2 == 0), jnp.logical_or(even, other % 2 == 1))
        direct = jnp.logical_or(apart, jnp.logical_or(is_hub, hub_of(other) == other))
        return jnp.logical_and(other != z, jnp.logical_or(other == buddy, direct))

    barrier = pltpu.get_barrier_semaphore()
    expected = 2 * (shots - 1) + 1 + jnp.where(is_hub, 0, shots - 1)
    for d in range(1, shots):
        for h in range(2):
            pl.semaphore_signal(barrier, inc=1, device_id=(lax.rem(s + d, shots), 2 * z + h), device_id_type=MESH)
    pl.semaphore_signal(barrier, inc=1, device_id=(s, partner), device_id_type=MESH)
    for other in range(chips):
        expected = expected + jnp.where(meets(other), 2, 0)

        @pl.when(meets(other))
        def _():
            for h in range(2):
                pl.semaphore_signal(barrier, inc=1, device_id=(s, 2 * other + h), device_id_type=MESH)

    @pl.when(gathers)
    def _():
        for d in range(1, shots):
            for h in range(2):
                pl.semaphore_signal(
                    barrier, inc=1, device_id=(lax.rem(s + d, shots), 2 * buddy + h), device_id_type=MESH
                )

    near[0].wait()
    build_filters(taps, lateral, depth)
    near[1].wait()
    near[2].wait()
    slot_at = lax.broadcasted_iota(jnp.int32, (1, slots), 1)
    for g in range(shots):
        for a in range(2):
            found = jnp.full((1, slots), panels, jnp.int32)
            for k in range(panels):
                found = jnp.where(slot_at == tile_slot[aperture[g, (2 * z + a) * panels + k]], k, found)
            table_vector[2 * g + a : 2 * g + a + 1, :] = found
    table_copy = pltpu.make_async_copy(table_vector, table, table_sem)
    table_copy.start()
    for i in range(2):
        for g in range(shots):
            for a in range(2):
                gathered[i][g, a, panels] = jnp.zeros((width, NZ), jnp.bfloat16)
                gathered_pair[i, g, a, panels] = jnp.zeros((width, NZ), jnp.bfloat16)

    @pl.when(is_hub)
    def _():
        final_in[pair, 1] = jnp.zeros((owned, width, NZ), jnp.bfloat16)

    @pl.when(jnp.logical_not(is_hub))
    def _():
        own_in[1] = jnp.zeros((owned, width, NZ), jnp.bfloat16)

    def channel(i):
        return 2 + core if i else 1 - core

    def foreign(c):
        return core == (0, 1, 1, 0)[c]

    def peer_of(d):
        if d == 1:
            return shots - 1 - s
        if d == 2:
            return lax.rem(s + 2, shots)
        return s + 1 - 2 * (s % 2) if d else s

    def shot_copy(c, d, first, count):
        peer = peer_of(d)
        return pltpu.make_async_remote_copy(
            src_ref=images.at[peer, c, pl.ds(first, count)],
            dst_ref=gathered[c // 2].at[s, core, pl.ds(first, count)],
            send_sem=shot_send.at[c, d],
            recv_sem=shot_recv.at[c // 2, d, core],
            device_id=(peer, 2 * z + (1, 0, 0, 1)[c] if d else partner),
            device_id_type=MESH,
        )

    def shot_start(c, first, count):
        for d in range(1, shots):
            shot_copy(c, d, first, count).start()

        @pl.when(foreign(c))
        def _():
            shot_copy(c, 0, first, count).start()

    def pair_copy(d, first, count):
        peer = peer_of(d)
        return pltpu.make_async_remote_copy(
            src_ref=images.at[peer, 1, pl.ds(first, count)],
            dst_ref=gathered_pair.at[side, s, core, pl.ds(first, count)],
            send_sem=shot_send.at[1, d],
            recv_sem=pair_recv.at[d, side, core],
            device_id=(peer, 2 * hub),
            device_id_type=MESH,
        )

    def pair_start(first, count):
        @pl.when(jnp.logical_not(gathers))
        def _():
            pair_copy(0, first, count).start()

        for d in range(1, shots):
            pair_copy(d, first, count).start()

    def pair_wait(d, from_side, a):
        return pltpu.make_async_remote_copy(
            src_ref=images.at[0, 0],
            dst_ref=gathered_pair.at[from_side, peer_of(d), a, pl.ds(0, panels)],
            send_sem=shot_send.at[1, d],
            recv_sem=pair_recv.at[d, from_side, a],
            device_id=(s, partner),
            device_id_type=MESH,
        )

    def shot_wait(i, d, a):
        return pltpu.make_async_remote_copy(
            src_ref=images.at[0, 0],
            dst_ref=gathered[i].at[peer_of(d), a, pl.ds(0, panels)],
            send_sem=shot_send.at[0, d],
            recv_sem=shot_recv.at[i, d, a],
            device_id=(s, partner),
            device_id_type=MESH,
        )

    def parts(f, k, j, half):
        left, right = fields[f, k, 2 * j], fields[f, k, 2 * j + 1]
        both = jnp.concatenate([left.reshape(192, NZ), right.reshape(192, NZ)], axis=1)
        wide = both.astype(jnp.float32)
        some = jnp.concatenate([wide[8 * y : 8 * y + 8] for y in range(half, 24, 2)], axis=0).astype(jnp.bfloat16)
        flat = jnp.dot(lateral[half * 128 : half * 128 + 128], both, preferred_element_type=jnp.float32)
        deep = jnp.dot(some, depth[...], preferred_element_type=jnp.float32)
        return flat[0:32] + deep[64:96], flat[32:64] - deep[32:64], flat[64:96] + deep[0:32], flat[96:128]

    for half in range(2):
        batch = (2, 4)[half]
        last = panels // batch - 1

        @pl.loop(0, panels // batch)
        def _(q):
            if half == 0:
                for n in range(batch):
                    load(0, q * batch + n).wait()
                    load(1, q * batch + n).wait()
            for n in range(batch):
                k = q * batch + n
                sums = None
                for j in range(levels // 2):
                    a, a0, a1, a2 = parts(0, k, j, half)
                    b, b0, b1, b2 = parts(1, k, j, half)
                    new = (a * b, a * (b0 + b1 + b2), (a0 + a1 + a2) * b, a0 * b0 + a1 * b1 + a2 * b2)
                    sums = new if sums is None else tuple(x + y for x, y in zip(sums, new))
                image = [(total[:, :NZ] + total[:, NZ:]).reshape(shots, 8, NZ) for total in sums]
                images[:, 3 * half, k] = jnp.concatenate(image[:2], axis=1).astype(jnp.bfloat16)
                images[:, 1 + half, k] = jnp.concatenate(image[2:], axis=1).astype(jnp.bfloat16)
            if half == 0:
                @pl.when(q == last - 1)
                def _():
                    pl.semaphore_wait(barrier, expected)
                    shot_start(0, 0, panels - batch)

                @pl.when(q == last)
                def _():
                    shot_start(0, panels - batch, batch)

        if half == 0:
            pair_start(0, panels)
        else:
            shot_start(2, 0, panels)
            shot_start(3, 0, panels)
        gathered[half][s, core, 0:panels] = images[s, channel(half)]

    table_copy.wait()

    @pl.when(gathers)
    def _():
        gathered_pair[side, s, 0, 0:panels] = images[s, 1]
        for n in range(2):
            for g in range(shots):
                for a in range(2):
                    found = jnp.full((1, slots), panels, jnp.int32)
                    for k in range(panels):
                        place = (2 * (2 * pair + n) + a) * panels + k
                        found = jnp.where(slot_at == tile_slot[aperture[g, place]], k, found)
                    line = (n * shots + g) * 2 + a
                    pair_vector[line : line + 1, :] = found
        whole = pltpu.make_async_copy(pair_vector, pair_table, table_sem)
        whole.start()
        whole.wait()

    def combined(i, row):
        total = None
        for g in range(shots):
            for a in range(2):
                term = gathered[i][g, a, table[2 * g + a, row]].astype(jnp.float32)
                total = term if total is None else total + term
        return total

    def pair_combined(row):
        total = None
        for n in range(2):
            for g in range(shots):
                for a in range(2):
                    at = pair_table[(n * shots + g) * 2 + a, row]
                    term = gathered_pair[n, g, a, at].astype(jnp.float32)
                    total = term if total is None else total + term
        return total

    def pair_final(block, o):
        return pltpu.make_async_remote_copy(
            src_ref=line_pair.at[block, pl.ds(o * owned, owned)],
            dst_ref=final_in.at[pair, 1],
            send_sem=pair_send.at[block, o],
            recv_sem=final_recv.at[pair, 1],
            device_id=(s, 2 * block + o),
            device_id_type=MESH,
        )

    def relay_copy(i, block, o):
        return pltpu.make_async_remote_copy(
            src_ref=line_out.at[i, block, pl.ds(o * owned, owned)],
            dst_ref=relay_in.at[i, block, pl.ds(o * owned, owned)],
            send_sem=relay_send.at[i, block, o],
            recv_sem=relay_recv.at[i, block, o],
            device_id=(s, 2 * buddy + core),
            device_id_type=MESH,
        )

    def final_copy(i, block, o):
        c = channel(i)
        return pltpu.make_async_remote_copy(
            src_ref=line_out.at[i, block, pl.ds(o * owned, owned)],
            dst_ref=final_in.at[z // 2, c],
            send_sem=final_send.at[i, block, o],
            recv_sem=final_recv.at[z // 2, c],
            device_id=(s, 2 * block + o),
            device_id_type=MESH,
        )

    def final_wait(p, c):
        return pltpu.make_async_remote_copy(
            src_ref=line_out.at[0, 0, pl.ds(0, owned)],
            dst_ref=final_in.at[p, c],
            send_sem=final_send.at[0, 0, 0],
            recv_sem=final_recv.at[p, c],
            device_id=(s, partner),
            device_id_type=MESH,
        )

    def own_copy(i):
        return pltpu.make_async_remote_copy(
            src_ref=own_out.at[i],
            dst_ref=own_in.at[channel(i)],
            send_sem=own_send.at[i],
            recv_sem=own_recv.at[i],
            device_id=(s, partner),
            device_id_type=MESH,
        )

    def toward(block):
        return jnp.where(even, block > z, block < z)

    def arrived(i):
        for d in range(1, shots):
            for a in range(2):
                shot_wait(i, d, a).wait_recv()
        shot_wait(i, 0, 1 - core).wait_recv()

    def far(i):
        @pl.loop(0, chips)
        def _(j):
            block = jnp.where(even, chips - 1 - j, j)

            @pl.when(jnp.logical_and(toward(block), block != buddy))
            def _():
                for o in range(2):
                    for r in range(o * owned, (o + 1) * owned):
                        line_out[i, block, r] = combined(i, 2 * block * owned + r).astype(jnp.bfloat16)
                    relay_copy(i, block, o).start()

    def near_by(i):
        for o in range(2):
            for r in range(o * owned, (o + 1) * owned):
                line_out[i, buddy, r] = combined(i, 2 * buddy * owned + r).astype(jnp.bfloat16)
            final_copy(i, buddy, o).start()

    def here(i):
        for r in range(owned):
            own_out[i, r] = combined(i, (2 * z + 1 - core) * owned + r).astype(jnp.bfloat16)
        own_copy(i).start()
        for r in range(owned):
            own_in[channel(i), r] = combined(i, t * owned + r).astype(jnp.bfloat16)

    def relay(i):
        @pl.loop(0, chips)
        def _(j):
            block = jnp.where(even, j, chips - 1 - j)

            @pl.when(jnp.logical_and(block != z, jnp.logical_not(toward(block))))
            def _():
                for o in range(2):
                    relay_copy(i, block, o).wait_recv()
                    for r in range(o * owned, (o + 1) * owned):
                        total = combined(i, 2 * block * owned + r) + relay_in[i, block, r].astype(jnp.float32)
                        line_out[i, block, r] = total.astype(jnp.bfloat16)
                    final_copy(i, block, o).start()

    def finish(c):
        if c == 1:
            @pl.when(jnp.logical_and(is_hub, core == 1))
            def _():
                own_copy(0).wait_recv()
        else:
            @pl.when(foreign(c))
            def _():
                own_copy(c // 2).wait_recv()

        for p in range(chips // 2):
            if c == 1:
                @pl.when(jnp.logical_or(p != pair, jnp.logical_not(is_hub)))
                def _():
                    final_wait(p, c).wait_recv()
            else:
                final_wait(p, c).wait_recv()
        for r in range(owned):
            total = own_in[c, r].astype(jnp.float32)
            for p in range(chips // 2):
                total = total + final_in[p, c, r].astype(jnp.float32)
            near_y = slice(c // 2 * 8, c // 2 * 8 + 8)
            for kind in range(2):
                image = kind if c in (0, 3) else kind + 2
                out[r, image, near_y] = factor[(0, 1, 1, 2)[image], r, near_y] * total[kind * 8 : kind * 8 + 8]

    def gather_pair():
        for d in range(shots):
            for a in range(2):
                if d or a:
                    pair_wait(d, 0, a).wait_recv()
                    pair_wait(d, 1, a).wait_recv()
        pair_wait(0, 1 - side, 0).wait_recv()

        @pl.loop(0, chips)
        def _(j):
            block = jnp.where(even, j, chips - 1 - j)

            @pl.when(block != z)
            def _():
                for o in range(2):
                    for r in range(o * owned, (o + 1) * owned):
                        line_pair[block, r] = pair_combined(2 * block * owned + r).astype(jnp.bfloat16)
                    pair_final(block, o).start()

        for r in range(owned):
            own_out[0, r] = pair_combined((2 * z + 1) * owned + r).astype(jnp.bfloat16)
        own_copy(0).start()
        for r in range(owned):
            own_in[1, r] = pair_combined(2 * z * owned + r).astype(jnp.bfloat16)

    @pl.when(core == 1)
    def _():
        arrived(0)
        far(0)
        near_by(0)
        here(0)
        relay(0)

    near[3].wait()
    rows = pl.ds(pl.multiple_of(s * width, width), width)
    for r in range(owned):
        speed_p = model[r, 0, rows].astype(jnp.float32)
        speed_s = model[r, 1, rows].astype(jnp.float32)
        shear = model[r, 2, rows].astype(jnp.float32) * speed_s
        factor[0, r] = model[r, 2, rows].astype(jnp.float32) * speed_p
        factor[1, r] = shear
        factor[2, r] = shear * speed_s / speed_p
    pl.when(gathers)(gather_pair)
    arrived(1)
    far(1)
    near_by(1)
    here(1)
    relay(1)
    for c in range(4):
        finish(c)

    for c in (0, 2, 3):
        for d in range(1, shots):
            shot_copy(c, d, 0, panels).wait_send()

        @pl.when(foreign(c))
        def _():
            shot_copy(c, 0, 0, panels).wait_send()

    for d in range(1, shots):
        pair_copy(d, 0, panels).wait_send()

    @pl.when(jnp.logical_not(gathers))
    def _():
        pair_copy(0, 0, panels).wait_send()

    @pl.when(gathers)
    def _():
        own_copy(0).wait_send()

        @pl.loop(0, chips)
        def _(block):
            @pl.when(block != z)
            def _():
                pair_final(block, 0).wait_send()
                pair_final(block, 1).wait_send()

    def sent(i):
        own_copy(i).wait_send()

        @pl.loop(0, chips)
        def _(block):
            relayed = jnp.logical_and(toward(block), block != buddy)

            @pl.when(relayed)
            def _():
                relay_copy(i, block, 0).wait_send()
                relay_copy(i, block, 1).wait_send()

            @pl.when(jnp.logical_and(block != z, jnp.logical_not(relayed)))
            def _():
                final_copy(i, block, 0).wait_send()
                final_copy(i, block, 1).wait_send()

    pl.when(core == 1)(lambda: sent(0))
    sent(1)


def tall(array):
    lead = array.shape[:-2]
    wide = array.shape[-1] // NZ
    array = array.reshape(lead + (8, wide, NZ))
    return jnp.swapaxes(array, -3, -2).reshape(lead + (8 * wide, NZ))


def body(src_field, rcv_field, model_panels, deriv_taps, aperture, tile_slot):
    tiles = lax.axis_size("tile")
    shots = lax.axis_size("shot")
    owned = model_panels.shape[0]
    panels, levels = src_field.shape[3], src_field.shape[1]
    chips = tiles // 2
    slots = tiles * owned
    width = 64 // shots

    vmem = pl.BlockSpec(memory_space=pltpu.VMEM)
    hbm = pl.BlockSpec(memory_space=pltpu.HBM)
    line = (2, chips, 2 * owned, width, NZ)
    result = pl.pallas_call(
        functools.partial(kernel, shots, tiles),
        out_shape=pltpu.VMEM((owned, 4, width, NZ), jnp.float32),
        in_specs=[hbm] * 6,
        out_specs=vmem,
        scratch_shapes=[
            pltpu.VMEM((2, panels, levels, 3, 64, NZ), jnp.bfloat16),
            pltpu.VMEM((256, 192), jnp.bfloat16),
            pltpu.VMEM((2 * NZ, 2 * NZ), jnp.bfloat16),
            pltpu.VMEM((shots, 4, panels, width, NZ), jnp.bfloat16),
            pltpu.VMEM((shots, 2, panels + 1, width, NZ), jnp.bfloat16),
            pltpu.VMEM((shots, 2, panels + 1, width, NZ), jnp.bfloat16),
            pltpu.VMEM((2, shots, 2, panels + 1, width, NZ), jnp.bfloat16),
            pltpu.VMEM(line, jnp.bfloat16),
            pltpu.VMEM(line[1:], jnp.bfloat16),
            pltpu.VMEM(line, jnp.bfloat16),
            pltpu.VMEM((chips // 2, 4, owned, width, NZ), jnp.bfloat16),
            pltpu.VMEM((2, owned, width, NZ), jnp.bfloat16),
            pltpu.VMEM((4, owned, width, NZ), jnp.bfloat16),
            pltpu.SemaphoreType.DMA((2, panels)),
            pltpu.SemaphoreType.DMA((4, shots)),
            pltpu.SemaphoreType.DMA((2, shots, 2)),
            pltpu.SemaphoreType.DMA((shots, 2, 2)),
            pltpu.SemaphoreType.DMA((2, chips, 2)),
            pltpu.SemaphoreType.DMA((2, chips, 2)),
            pltpu.SemaphoreType.DMA((2, chips, 2)),
            pltpu.SemaphoreType.DMA((chips, 2)),
            pltpu.SemaphoreType.DMA((chips // 2, 4)),
            pltpu.SemaphoreType.DMA((2,)),
            pltpu.SemaphoreType.DMA((2,)),
            pltpu.VMEM((2 * shots, slots), jnp.int32),
            pltpu.SMEM((2 * shots, slots), jnp.int32),
            pltpu.SemaphoreType.DMA,
            pltpu.VMEM((4 * shots, slots), jnp.int32),
            pltpu.SMEM((4 * shots, slots), jnp.int32),
            pltpu.SMEM(deriv_taps.shape, jnp.float32),
            pltpu.SMEM(aperture.shape, jnp.int32),
            pltpu.SMEM(tile_slot.shape, jnp.int32),
            pltpu.VMEM((owned, 3, 64, NZ), jnp.bfloat16),
            pltpu.SemaphoreType.DMA((4,)),
            pltpu.VMEM((3, owned, width, NZ), jnp.float32),
        ],
        compiler_params=pltpu.CompilerParams(collective_id=0, has_side_effects=True, vmem_limit_bytes=48 * 1024 * 1024),
    )(*[pltpu.with_memory_space_constraint(v, pltpu.HBM) for v in (deriv_taps, aperture, tile_slot, tall(src_field[0]), tall(rcv_field[0]), tall(model_panels))])

    def spill(near, far, sem):
        copies = [pltpu.make_async_copy(near.at[r], far.at[r], sem.at[r]) for r in range(owned)]
        for copy in copies:
            copy.start()
        for copy in copies:
            copy.wait()

    wide = jnp.swapaxes(result.reshape(owned, 4, width // 8, 8, NZ), 2, 3)
    return wide.reshape(owned, 4, 8, (width // 8) * NZ)


def solution(mesh):
    return jax.shard_map(
        body,
        mesh=mesh,
        in_specs=(
            P("shot", None, None, "tile", None, None),
            P("shot", None, None, "tile", None, None),
            P("tile", None, None, None),
            P(),
            P(),
            P(),
        ),
        out_specs=P("tile", None, None, "shot"),
        check_vma=False,
    )
```

```python
import functools

import jax
import jax.numpy as jnp
from jax import lax
from jax.experimental import pallas as pl
from jax.experimental.pallas import tpu as pltpu
from jax.sharding import PartitionSpec as P

MESH = pl.DeviceIdType.MESH
TAPS = 16
NZ = 128


def tap_values(taps, axis, offset):
    total = jnp.zeros(offset.shape, jnp.float32)
    for tap in range(TAPS):
        total = jnp.where(offset == tap, taps[axis, tap], total)
    return total


def build_filters(taps, lateral, depth):
    rows = lax.broadcasted_iota(jnp.int32, (32, 64), 0)
    cols = lax.broadcasted_iota(jnp.int32, (32, 64), 1)
    none = jnp.zeros((32, 64), jnp.float32)
    for half in range(2):
        at_y = 2 * (rows // 8) + half
        along_x = jnp.where(at_y == cols // 8, tap_values(taps, 0, cols % 8 - rows % 8 + 8), 0.0)
        along_y = jnp.where(rows % 8 == cols % 8, tap_values(taps, 1, cols // 8 - at_y + 8), 0.0)
        table = (
            (along_x, along_y, none),
            (none, none, along_y),
            (none, none, -along_x),
            (-along_y, along_x, none),
        )
        for out, line in enumerate(table):
            first = half * 128 + out * 32
            lateral[first : first + 32, :] = jnp.concatenate(line, axis=1).astype(jnp.bfloat16)
    rows = lax.broadcasted_iota(jnp.int32, (NZ, NZ), 0)
    cols = lax.broadcasted_iota(jnp.int32, (NZ, NZ), 1)
    along_z = tap_values(taps, 2, rows - cols + 8).astype(jnp.bfloat16)
    zeros = jnp.zeros((NZ, NZ), jnp.bfloat16)
    depth[:NZ, :NZ] = along_z
    depth[:NZ, NZ:] = zeros
    depth[NZ:, :NZ] = zeros
    depth[NZ:, NZ:] = along_z


def kernel(shots, tiles, taps_far, aperture_far, tile_slot_far, src, rcv, model_far, out, fields, lateral, depth, images, gathered_first, gathered_second, gathered_pair,
           line_out, line_pair, relay_in, final_in, own_out, own_in, load_sem, shot_send, shot_recv, pair_recv, relay_send, relay_recv,
           final_send, pair_send, final_recv, own_send, own_recv, table_vector, table, table_sem, pair_vector, pair_table,
           taps, aperture, tile_slot, model, near_sem, factor):
    s = lax.axis_index("shot")
    t = lax.axis_index("tile")
    chips = tiles // 2
    z, core = t // 2, t % 2
    even = z % 2 == 0
    buddy = z + 1 - 2 * (z % 2)
    partner = t + 1 - 2 * core
    panels, levels = fields.shape[1], fields.shape[2]
    owned = out.shape[0]
    slots = tiles * owned
    part = owned // 2
    width = 64 // shots
    gathered = (gathered_first, gathered_second)
    pair, side = z // 2, z % 2

    def hub_of(chip):
        return chip // 2 * 2 + jnp.where(chip // 2 < chips // 4, 1, 0)

    hub = hub_of(z)
    is_hub = z == hub
    gathers = jnp.logical_and(is_hub, core == 0)

    def load(f, k):
        return pltpu.make_async_copy((src, rcv)[f].at[:, :, k], fields.at[f, k], load_sem.at[f, k])

    near = [
        pltpu.make_async_copy(far, ref, near_sem.at[i])
        for i, (far, ref) in enumerate(
            ((taps_far, taps), (aperture_far, aperture), (tile_slot_far, tile_slot), (model_far, model))
        )
    ]
    for copy in near[:3]:
        copy.start()

    @pl.loop(0, panels)
    def _(k):
        load(0, k).start()
        load(1, k).start()

    near[3].start()

    def meets(other):
        apart = jnp.where(other > z, jnp.logical_or(z % 2 == 1, other % 2 == 0), jnp.logical_or(even, other % 2 == 1))
        direct = jnp.logical_or(apart, jnp.logical_or(is_hub, hub_of(other) == other))
        return jnp.logical_and(other != z, jnp.logical_or(other == buddy, direct))

    barrier = pltpu.get_barrier_semaphore()
    expected = 2 * (shots - 1) + 1 + jnp.where(is_hub, 0, shots - 1)
    for d in range(1, shots):
        for h in range(2):
            pl.semaphore_signal(barrier, inc=1, device_id=(lax.rem(s + d, shots), 2 * z + h), device_id_type=MESH)
    pl.semaphore_signal(barrier, inc=1, device_id=(s, partner), device_id_type=MESH)
    for other in range(chips):
        expected = expected + jnp.where(meets(other), 2, 0)

        @pl.when(meets(other))
        def _():
            for h in range(2):
                pl.semaphore_signal(barrier, inc=1, device_id=(s, 2 * other + h), device_id_type=MESH)

    @pl.when(gathers)
    def _():
        for d in range(1, shots):
            for h in range(2):
                pl.semaphore_signal(
                    barrier, inc=1, device_id=(lax.rem(s + d, shots), 2 * buddy + h), device_id_type=MESH
                )

    near[0].wait()
    build_filters(taps, lateral, depth)
    near[1].wait()
    near[2].wait()
    slot_at = lax.broadcasted_iota(jnp.int32, (1, slots), 1)
    for g in range(shots):
        for a in range(2):
            found = jnp.full((1, slots), panels, jnp.int32)
            for k in range(panels):
                found = jnp.where(slot_at == tile_slot[aperture[g, (2 * z + a) * panels + k]], k, found)
            table_vector[2 * g + a : 2 * g + a + 1, :] = found
    table_copy = pltpu.make_async_copy(table_vector, table, table_sem)
    table_copy.start()
    for i in range(2):
        for g in range(shots):
            for a in range(2):
                gathered[i][g, a, panels] = jnp.zeros((width, NZ), jnp.bfloat16)
                gathered_pair[i, g, a, panels] = jnp.zeros((width, NZ), jnp.bfloat16)

    @pl.when(is_hub)
    def _():
        final_in[pair, 1] = jnp.zeros((owned, width, NZ), jnp.bfloat16)

    @pl.when(jnp.logical_not(is_hub))
    def _():
        own_in[1] = jnp.zeros((owned, width, NZ), jnp.bfloat16)

    def channel(i):
        return 2 + core if i else 1 - core

    def foreign(c):
        return core == (0, 1, 1, 0)[c]

    def peer_of(d):
        if d == 1:
            return shots - 1 - s
        if d == 2:
            return lax.rem(s + 2, shots)
        return s + 1 - 2 * (s % 2) if d else s

    def shot_copy(c, d, first, count):
        peer = peer_of(d)
        return pltpu.make_async_remote_copy(
            src_ref=images.at[peer, c, pl.ds(first, count)],
            dst_ref=gathered[c // 2].at[s, core, pl.ds(first, count)],
            send_sem=shot_send.at[c, d],
            recv_sem=shot_recv.at[c // 2, d, core],
            device_id=(peer, 2 * z + (1, 0, 0, 1)[c] if d else partner),
            device_id_type=MESH,
        )

    def shot_start(c, first, count):
        for d in range(1, shots):
            shot_copy(c, d, first, count).start()

        @pl.when(foreign(c))
        def _():
            shot_copy(c, 0, first, count).start()

    def pair_copy(d, first, count):
        peer = peer_of(d)
        return pltpu.make_async_remote_copy(
            src_ref=images.at[peer, 1, pl.ds(first, count)],
            dst_ref=gathered_pair.at[side, s, core, pl.ds(first, count)],
            send_sem=shot_send.at[1, d],
            recv_sem=pair_recv.at[d, side, core],
            device_id=(peer, 2 * hub),
            device_id_type=MESH,
        )

    def pair_start(first, count):
        @pl.when(jnp.logical_not(gathers))
        def _():
            pair_copy(0, first, count).start()

        for d in range(1, shots):
            pair_copy(d, first, count).start()

    def pair_wait(d, from_side, a):
        return pltpu.make_async_remote_copy(
            src_ref=images.at[0, 0],
            dst_ref=gathered_pair.at[from_side, peer_of(d), a, pl.ds(0, panels)],
            send_sem=shot_send.at[1, d],
            recv_sem=pair_recv.at[d, from_side, a],
            device_id=(s, partner),
            device_id_type=MESH,
        )

    def shot_wait(i, d, a):
        return pltpu.make_async_remote_copy(
            src_ref=images.at[0, 0],
            dst_ref=gathered[i].at[peer_of(d), a, pl.ds(0, panels)],
            send_sem=shot_send.at[0, d],
            recv_sem=shot_recv.at[i, d, a],
            device_id=(s, partner),
            device_id_type=MESH,
        )

    def parts(f, k, j, half):
        left, right = fields[f, k, 2 * j], fields[f, k, 2 * j + 1]
        both = jnp.concatenate([left.reshape(192, NZ), right.reshape(192, NZ)], axis=1)
        wide = both.astype(jnp.float32)
        some = jnp.concatenate([wide[8 * y : 8 * y + 8] for y in range(half, 24, 2)], axis=0).astype(jnp.bfloat16)
        flat = jnp.dot(lateral[half * 128 : half * 128 + 128], both, preferred_element_type=jnp.float32)
        deep = jnp.dot(some, depth[...], preferred_element_type=jnp.float32)
        return flat[0:32] + deep[64:96], flat[32:64] - deep[32:64], flat[64:96] + deep[0:32], flat[96:128]

    for half in range(2):
        batch = (2, 4)[half]
        last = panels // batch - 1

        @pl.loop(0, panels // batch)
        def _(q):
            if half == 0:
                for n in range(batch):
                    load(0, q * batch + n).wait()
                    load(1, q * batch + n).wait()
            for n in range(batch):
                k = q * batch + n
                sums = None
                for j in range(levels // 2):
                    a, a0, a1, a2 = parts(0, k, j, half)
                    b, b0, b1, b2 = parts(1, k, j, half)
                    new = (a * b, a * (b0 + b1 + b2), (a0 + a1 + a2) * b, a0 * b0 + a1 * b1 + a2 * b2)
                    sums = new if sums is None else tuple(x + y for x, y in zip(sums, new))
                image = [(total[:, :NZ] + total[:, NZ:]).reshape(shots, 8, NZ) for total in sums]
                images[:, 3 * half, k] = jnp.concatenate(image[:2], axis=1).astype(jnp.bfloat16)
                images[:, 1 + half, k] = jnp.concatenate(image[2:], axis=1).astype(jnp.bfloat16)
            if half == 0:
                @pl.when(q == last - 1)
                def _():
                    pl.semaphore_wait(barrier, expected)
                    shot_start(0, 0, panels - batch)

                @pl.when(q == last)
                def _():
                    shot_start(0, panels - batch, batch)

        if half == 0:
            pair_start(0, panels)
        else:
            shot_start(2, 0, panels)
            shot_start(3, 0, panels)
        gathered[half][s, core, 0:panels] = images[s, channel(half)]

    table_copy.wait()

    @pl.when(gathers)
    def _():
        gathered_pair[side, s, 0, 0:panels] = images[s, 1]
        for n in range(2):
            for g in range(shots):
                for a in range(2):
                    found = jnp.full((1, slots), panels, jnp.int32)
                    for k in range(panels):
                        place = (2 * (2 * pair + n) + a) * panels + k
                        found = jnp.where(slot_at == tile_slot[aperture[g, place]], k, found)
                    line = (n * shots + g) * 2 + a
                    pair_vector[line : line + 1, :] = found
        whole = pltpu.make_async_copy(pair_vector, pair_table, table_sem)
        whole.start()
        whole.wait()

    def combined(i, row):
        total = None
        for g in range(shots):
            for a in range(2):
                term = gathered[i][g, a, table[2 * g + a, row]].astype(jnp.float32)
                total = term if total is None else total + term
        return total

    def pair_combined(row):
        total = None
        for n in range(2):
            for g in range(shots):
                for a in range(2):
                    at = pair_table[(n * shots + g) * 2 + a, row]
                    term = gathered_pair[n, g, a, at].astype(jnp.float32)
                    total = term if total is None else total + term
        return total

    def pair_final(block, o):
        return pltpu.make_async_remote_copy(
            src_ref=line_pair.at[block, pl.ds(o * owned, owned)],
            dst_ref=final_in.at[pair, 1],
            send_sem=pair_send.at[block, o],
            recv_sem=final_recv.at[pair, 1],
            device_id=(s, 2 * block + o),
            device_id_type=MESH,
        )

    def relay_copy(i, block, o):
        return pltpu.make_async_remote_copy(
            src_ref=line_out.at[i, block, pl.ds(o * part, part)],
            dst_ref=relay_in.at[i, block, pl.ds(o * part, part)],
            send_sem=relay_send.at[i, block, o],
            recv_sem=relay_recv.at[i, block, o],
            device_id=(s, 2 * buddy + core),
            device_id_type=MESH,
        )

    def final_copy(i, block, o):
        c = channel(i)
        return pltpu.make_async_remote_copy(
            src_ref=line_out.at[i, block, pl.ds(o * part, part)],
            dst_ref=final_in.at[z // 2, c, pl.ds(o % 2 * part, part)],
            send_sem=final_send.at[i, block, o],
            recv_sem=final_recv.at[z // 2, c],
            device_id=(s, 2 * block + o // 2),
            device_id_type=MESH,
        )

    def final_wait(p, c):
        return pltpu.make_async_remote_copy(
            src_ref=line_out.at[0, 0, pl.ds(0, owned)],
            dst_ref=final_in.at[p, c],
            send_sem=final_send.at[0, 0, 0],
            recv_sem=final_recv.at[p, c],
            device_id=(s, partner),
            device_id_type=MESH,
        )

    def own_copy(i):
        return pltpu.make_async_remote_copy(
            src_ref=own_out.at[i],
            dst_ref=own_in.at[channel(i)],
            send_sem=own_send.at[i],
            recv_sem=own_recv.at[i],
            device_id=(s, partner),
            device_id_type=MESH,
        )

    def toward(block):
        return jnp.where(even, block > z, block < z)

    def arrived(i):
        for d in range(1, shots):
            for a in range(2):
                shot_wait(i, d, a).wait_recv()
        shot_wait(i, 0, 1 - core).wait_recv()

    def far(i):
        @pl.loop(0, chips)
        def _(j):
            block = jnp.where(even, chips - 1 - j, j)

            @pl.when(jnp.logical_and(toward(block), block != buddy))
            def _():
                for o in range(4):
                    for r in range(o * part, (o + 1) * part):
                        line_out[i, block, r] = combined(i, 2 * block * owned + r).astype(jnp.bfloat16)
                    relay_copy(i, block, o).start()

    def near_by(i):
        for o in range(4):
            for r in range(o * part, (o + 1) * part):
                line_out[i, buddy, r] = combined(i, 2 * buddy * owned + r).astype(jnp.bfloat16)
            final_copy(i, buddy, o).start()

    def here(i):
        for r in range(owned):
            own_out[i, r] = combined(i, (2 * z + 1 - core) * owned + r).astype(jnp.bfloat16)
        own_copy(i).start()
        for r in range(owned):
            own_in[channel(i), r] = combined(i, t * owned + r).astype(jnp.bfloat16)

    def relay(i):
        @pl.loop(0, chips)
        def _(j):
            block = jnp.where(even, j, chips - 1 - j)

            @pl.when(jnp.logical_and(block != z, jnp.logical_not(toward(block))))
            def _():
                for o in range(4):
                    relay_copy(i, block, o).wait_recv()
                    for r in range(o * part, (o + 1) * part):
                        total = combined(i, 2 * block * owned + r) + relay_in[i, block, r].astype(jnp.float32)
                        line_out[i, block, r] = total.astype(jnp.bfloat16)
                    final_copy(i, block, o).start()

    def finish(c):
        if c == 1:
            @pl.when(jnp.logical_and(is_hub, core == 1))
            def _():
                own_copy(0).wait_recv()
        else:
            @pl.when(foreign(c))
            def _():
                own_copy(c // 2).wait_recv()

        for p in range(chips // 2):
            if c == 1:
                @pl.when(jnp.logical_or(p != pair, jnp.logical_not(is_hub)))
                def _():
                    final_wait(p, c).wait_recv()
            else:
                final_wait(p, c).wait_recv()
        for r in range(owned):
            total = own_in[c, r].astype(jnp.float32)
            for p in range(chips // 2):
                total = total + final_in[p, c, r].astype(jnp.float32)
            near_y = slice(c // 2 * 8, c // 2 * 8 + 8)
            for kind in range(2):
                image = kind if c in (0, 3) else kind + 2
                out[r, image, near_y] = factor[(0, 1, 1, 2)[image], r, near_y] * total[kind * 8 : kind * 8 + 8]

    def gather_pair():
        for d in range(shots):
            for a in range(2):
                if d or a:
                    pair_wait(d, 0, a).wait_recv()
                    pair_wait(d, 1, a).wait_recv()
        pair_wait(0, 1 - side, 0).wait_recv()

        @pl.loop(0, chips)
        def _(j):
            block = jnp.where(even, j, chips - 1 - j)

            @pl.when(block != z)
            def _():
                for o in range(2):
                    for r in range(o * owned, (o + 1) * owned):
                        line_pair[block, r] = pair_combined(2 * block * owned + r).astype(jnp.bfloat16)
                    pair_final(block, o).start()

        for r in range(owned):
            own_out[0, r] = pair_combined((2 * z + 1) * owned + r).astype(jnp.bfloat16)
        own_copy(0).start()
        for r in range(owned):
            own_in[1, r] = pair_combined(2 * z * owned + r).astype(jnp.bfloat16)

    @pl.when(core == 1)
    def _():
        arrived(0)
        far(0)
        near_by(0)
        here(0)
        relay(0)

    near[3].wait()
    rows = pl.ds(pl.multiple_of(s * width, width), width)
    for r in range(owned):
        speed_p = model[r, 0, rows].astype(jnp.float32)
        speed_s = model[r, 1, rows].astype(jnp.float32)
        shear = model[r, 2, rows].astype(jnp.float32) * speed_s
        factor[0, r] = model[r, 2, rows].astype(jnp.float32) * speed_p
        factor[1, r] = shear
        factor[2, r] = shear * speed_s / speed_p
    pl.when(gathers)(gather_pair)
    arrived(1)
    far(1)
    near_by(1)
    here(1)
    relay(1)
    for c in range(4):
        finish(c)

    for c in (0, 2, 3):
        for d in range(1, shots):
            shot_copy(c, d, 0, panels).wait_send()

        @pl.when(foreign(c))
        def _():
            shot_copy(c, 0, 0, panels).wait_send()

    for d in range(1, shots):
        pair_copy(d, 0, panels).wait_send()

    @pl.when(jnp.logical_not(gathers))
    def _():
        pair_copy(0, 0, panels).wait_send()

    @pl.when(gathers)
    def _():
        own_copy(0).wait_send()

        @pl.loop(0, chips)
        def _(block):
            @pl.when(block != z)
            def _():
                pair_final(block, 0).wait_send()
                pair_final(block, 1).wait_send()

    def sent(i):
        own_copy(i).wait_send()

        @pl.loop(0, chips)
        def _(block):
            relayed = jnp.logical_and(toward(block), block != buddy)

            @pl.when(relayed)
            def _():
                for o in range(4):
                    relay_copy(i, block, o).wait_send()

            @pl.when(jnp.logical_and(block != z, jnp.logical_not(relayed)))
            def _():
                for o in range(4):
                    final_copy(i, block, o).wait_send()

    pl.when(core == 1)(lambda: sent(0))
    sent(1)


def tall(array):
    lead = array.shape[:-2]
    wide = array.shape[-1] // NZ
    array = array.reshape(lead + (8, wide, NZ))
    return jnp.swapaxes(array, -3, -2).reshape(lead + (8 * wide, NZ))


def body(src_field, rcv_field, model_panels, deriv_taps, aperture, tile_slot):
    tiles = lax.axis_size("tile")
    shots = lax.axis_size("shot")
    owned = model_panels.shape[0]
    panels, levels = src_field.shape[3], src_field.shape[1]
    chips = tiles // 2
    slots = tiles * owned
    part = owned // 2
    width = 64 // shots

    vmem = pl.BlockSpec(memory_space=pltpu.VMEM)
    hbm = pl.BlockSpec(memory_space=pltpu.HBM)
    line = (2, chips, 2 * owned, width, NZ)
    result = pl.pallas_call(
        functools.partial(kernel, shots, tiles),
        out_shape=pltpu.VMEM((owned, 4, width, NZ), jnp.float32),
        in_specs=[hbm] * 6,
        out_specs=vmem,
        scratch_shapes=[
            pltpu.VMEM((2, panels, levels, 3, 64, NZ), jnp.bfloat16),
            pltpu.VMEM((256, 192), jnp.bfloat16),
            pltpu.VMEM((2 * NZ, 2 * NZ), jnp.bfloat16),
            pltpu.VMEM((shots, 4, panels, width, NZ), jnp.bfloat16),
            pltpu.VMEM((shots, 2, panels + 1, width, NZ), jnp.bfloat16),
            pltpu.VMEM((shots, 2, panels + 1, width, NZ), jnp.bfloat16),
            pltpu.VMEM((2, shots, 2, panels + 1, width, NZ), jnp.bfloat16),
            pltpu.VMEM(line, jnp.bfloat16),
            pltpu.VMEM(line[1:], jnp.bfloat16),
            pltpu.VMEM(line, jnp.bfloat16),
            pltpu.VMEM((chips // 2, 4, owned, width, NZ), jnp.bfloat16),
            pltpu.VMEM((2, owned, width, NZ), jnp.bfloat16),
            pltpu.VMEM((4, owned, width, NZ), jnp.bfloat16),
            pltpu.SemaphoreType.DMA((2, panels)),
            pltpu.SemaphoreType.DMA((4, shots)),
            pltpu.SemaphoreType.DMA((2, shots, 2)),
            pltpu.SemaphoreType.DMA((shots, 2, 2)),
            pltpu.SemaphoreType.DMA((2, chips, 4)),
            pltpu.SemaphoreType.DMA((2, chips, 4)),
            pltpu.SemaphoreType.DMA((2, chips, 4)),
            pltpu.SemaphoreType.DMA((chips, 2)),
            pltpu.SemaphoreType.DMA((chips // 2, 4)),
            pltpu.SemaphoreType.DMA((2,)),
            pltpu.SemaphoreType.DMA((2,)),
            pltpu.VMEM((2 * shots, slots), jnp.int32),
            pltpu.SMEM((2 * shots, slots), jnp.int32),
            pltpu.SemaphoreType.DMA,
            pltpu.VMEM((4 * shots, slots), jnp.int32),
            pltpu.SMEM((4 * shots, slots), jnp.int32),
            pltpu.SMEM(deriv_taps.shape, jnp.float32),
            pltpu.SMEM(aperture.shape, jnp.int32),
            pltpu.SMEM(tile_slot.shape, jnp.int32),
            pltpu.VMEM((owned, 3, 64, NZ), jnp.bfloat16),
            pltpu.SemaphoreType.DMA((4,)),
            pltpu.VMEM((3, owned, width, NZ), jnp.float32),
        ],
        compiler_params=pltpu.CompilerParams(collective_id=0, has_side_effects=True, vmem_limit_bytes=48 * 1024 * 1024),
    )(*[pltpu.with_memory_space_constraint(v, pltpu.HBM) for v in (deriv_taps, aperture, tile_slot, tall(src_field[0]), tall(rcv_field[0]), tall(model_panels))])

    def spill(near, far, sem):
        copies = [pltpu.make_async_copy(near.at[r], far.at[r], sem.at[r]) for r in range(owned)]
        for copy in copies:
            copy.start()
        for copy in copies:
            copy.wait()

    wide = jnp.swapaxes(result.reshape(owned, 4, width // 8, 8, NZ), 2, 3)
    return wide.reshape(owned, 4, 8, (width // 8) * NZ)


def solution(mesh):
    return jax.shard_map(
        body,
        mesh=mesh,
        in_specs=(
            P("shot", None, None, "tile", None, None),
            P("shot", None, None, "tile", None, None),
            P("tile", None, None, None),
            P(),
            P(),
            P(),
        ),
        out_specs=P("tile", None, None, "shot"),
        check_vma=False,
    )
```

```python
import functools

import jax
import jax.numpy as jnp
from jax import lax
from jax.experimental import pallas as pl
from jax.experimental.pallas import tpu as pltpu
from jax.sharding import PartitionSpec as P

MESH = pl.DeviceIdType.MESH
TAPS = 16
NZ = 128


def tap_values(taps, axis, offset):
    total = jnp.zeros(offset.shape, jnp.float32)
    for tap in range(TAPS):
        total = jnp.where(offset == tap, taps[axis, tap], total)
    return total


def build_filters(taps, lateral, depth):
    rows = lax.broadcasted_iota(jnp.int32, (32, 64), 0)
    cols = lax.broadcasted_iota(jnp.int32, (32, 64), 1)
    none = jnp.zeros((32, 64), jnp.float32)
    for half in range(2):
        at_y = 2 * (rows // 8) + half
        along_x = jnp.where(at_y == cols // 8, tap_values(taps, 0, cols % 8 - rows % 8 + 8), 0.0)
        along_y = jnp.where(rows % 8 == cols % 8, tap_values(taps, 1, cols // 8 - at_y + 8), 0.0)
        table = (
            (along_x, along_y, none),
            (none, none, along_y),
            (none, none, -along_x),
            (-along_y, along_x, none),
        )
        for out, line in enumerate(table):
            first = half * 128 + out * 32
            lateral[first : first + 32, :] = jnp.concatenate(line, axis=1).astype(jnp.bfloat16)
    rows = lax.broadcasted_iota(jnp.int32, (NZ, NZ), 0)
    cols = lax.broadcasted_iota(jnp.int32, (NZ, NZ), 1)
    along_z = tap_values(taps, 2, rows - cols + 8).astype(jnp.bfloat16)
    zeros = jnp.zeros((NZ, NZ), jnp.bfloat16)
    depth[:NZ, :NZ] = along_z
    depth[:NZ, NZ:] = zeros
    depth[NZ:, :NZ] = zeros
    depth[NZ:, NZ:] = along_z


def kernel(shots, tiles, taps_far, aperture_far, tile_slot_far, src, rcv, model_far, out, fields, lateral, depth, images, gathered_first, gathered_second, gathered_pair,
           line_out, line_pair, relay_in, final_in, own_out, own_in, load_sem, shot_send, shot_recv, pair_recv, relay_send, relay_recv,
           final_send, pair_send, final_recv, own_send, own_recv, table_vector, table, table_sem, pair_vector, pair_table,
           taps, aperture, tile_slot, model, near_sem, factor):
    s = lax.axis_index("shot")
    t = lax.axis_index("tile")
    chips = tiles // 2
    z, core = t // 2, t % 2
    even = z % 2 == 0
    buddy = z + 1 - 2 * (z % 2)
    partner = t + 1 - 2 * core
    panels, levels = fields.shape[1], fields.shape[2]
    owned = out.shape[0]
    slots = tiles * owned
    width = 64 // shots
    gathered = (gathered_first, gathered_second)
    pair, side = z // 2, z % 2

    def hub_of(chip):
        return chip // 2 * 2 + jnp.where(chip // 2 < chips // 4, 1, 0)

    hub = hub_of(z)
    is_hub = z == hub
    gathers = jnp.logical_and(is_hub, core == 0)

    def load(f, k):
        return pltpu.make_async_copy((src, rcv)[f].at[:, :, k], fields.at[f, k], load_sem.at[f, k])

    near = [
        pltpu.make_async_copy(far, ref, near_sem.at[i])
        for i, (far, ref) in enumerate(
            ((taps_far, taps), (aperture_far, aperture), (tile_slot_far, tile_slot), (model_far, model))
        )
    ]
    for copy in near[:3]:
        copy.start()

    @pl.loop(0, panels)
    def _(k):
        load(0, k).start()
        load(1, k).start()

    near[3].start()

    def meets(other):
        apart = jnp.where(other > z, jnp.logical_or(z % 2 == 1, other % 2 == 0), jnp.logical_or(even, other % 2 == 1))
        direct = jnp.logical_or(apart, jnp.logical_or(is_hub, hub_of(other) == other))
        return jnp.logical_and(other != z, jnp.logical_or(other == buddy, direct))

    barrier = pltpu.get_barrier_semaphore()
    expected = 2 * (shots - 1) + 1 + jnp.where(is_hub, 0, shots - 1)
    for d in range(1, shots):
        for h in range(2):
            pl.semaphore_signal(barrier, inc=1, device_id=(lax.rem(s + d, shots), 2 * z + h), device_id_type=MESH)
    pl.semaphore_signal(barrier, inc=1, device_id=(s, partner), device_id_type=MESH)
    for other in range(chips):
        expected = expected + jnp.where(meets(other), 2, 0)

        @pl.when(meets(other))
        def _():
            for h in range(2):
                pl.semaphore_signal(barrier, inc=1, device_id=(s, 2 * other + h), device_id_type=MESH)

    @pl.when(gathers)
    def _():
        for d in range(1, shots):
            for h in range(2):
                pl.semaphore_signal(
                    barrier, inc=1, device_id=(lax.rem(s + d, shots), 2 * buddy + h), device_id_type=MESH
                )

    near[0].wait()
    build_filters(taps, lateral, depth)
    near[1].wait()
    near[2].wait()
    slot_at = lax.broadcasted_iota(jnp.int32, (1, slots), 1)
    for g in range(shots):
        for a in range(2):
            found = jnp.full((1, slots), panels, jnp.int32)
            for k in range(panels):
                found = jnp.where(slot_at == tile_slot[aperture[g, (2 * z + a) * panels + k]], k, found)
            table_vector[2 * g + a : 2 * g + a + 1, :] = found
    table_copy = pltpu.make_async_copy(table_vector, table, table_sem)
    table_copy.start()
    for i in range(2):
        for g in range(shots):
            for a in range(2):
                gathered[i][g, a, panels] = jnp.zeros((width, NZ), jnp.bfloat16)
                gathered_pair[i, g, a, panels] = jnp.zeros((width, NZ), jnp.bfloat16)

    @pl.when(is_hub)
    def _():
        final_in[pair, 1] = jnp.zeros((owned, width, NZ), jnp.bfloat16)

    @pl.when(jnp.logical_not(is_hub))
    def _():
        own_in[1] = jnp.zeros((owned, width, NZ), jnp.bfloat16)

    def channel(i):
        return 2 + core if i else 1 - core

    def foreign(c):
        return core == (0, 1, 1, 0)[c]

    def peer_of(d):
        if d == 1:
            return shots - 1 - s
        if d == 2:
            return lax.rem(s + 2, shots)
        return s + 1 - 2 * (s % 2) if d else s

    def shot_copy(c, d, first, count):
        peer = peer_of(d)
        return pltpu.make_async_remote_copy(
            src_ref=images.at[peer, c, pl.ds(first, count)],
            dst_ref=gathered[c // 2].at[s, core, pl.ds(first, count)],
            send_sem=shot_send.at[c, d],
            recv_sem=shot_recv.at[c // 2, d, core],
            device_id=(peer, 2 * z + (1, 0, 0, 1)[c] if d else partner),
            device_id_type=MESH,
        )

    def shot_start(c, first, count):
        for d in range(1, shots):
            shot_copy(c, d, first, count).start()

        @pl.when(foreign(c))
        def _():
            shot_copy(c, 0, first, count).start()

    def pair_copy(d, first, count):
        peer = peer_of(d)
        return pltpu.make_async_remote_copy(
            src_ref=images.at[peer, 1, pl.ds(first, count)],
            dst_ref=gathered_pair.at[side, s, core, pl.ds(first, count)],
            send_sem=shot_send.at[1, d],
            recv_sem=pair_recv.at[d, side, core],
            device_id=(peer, 2 * hub),
            device_id_type=MESH,
        )

    def pair_start(first, count):
        @pl.when(jnp.logical_not(gathers))
        def _():
            pair_copy(0, first, count).start()

        for d in range(1, shots):
            pair_copy(d, first, count).start()

    def pair_wait(d, from_side, a):
        return pltpu.make_async_remote_copy(
            src_ref=images.at[0, 0],
            dst_ref=gathered_pair.at[from_side, peer_of(d), a, pl.ds(0, panels)],
            send_sem=shot_send.at[1, d],
            recv_sem=pair_recv.at[d, from_side, a],
            device_id=(s, partner),
            device_id_type=MESH,
        )

    def shot_wait(i, d, a):
        return pltpu.make_async_remote_copy(
            src_ref=images.at[0, 0],
            dst_ref=gathered[i].at[peer_of(d), a, pl.ds(0, panels)],
            send_sem=shot_send.at[0, d],
            recv_sem=shot_recv.at[i, d, a],
            device_id=(s, partner),
            device_id_type=MESH,
        )

    def parts(f, k, j, half):
        left, right = fields[f, k, 2 * j], fields[f, k, 2 * j + 1]
        both = jnp.concatenate([left.reshape(192, NZ), right.reshape(192, NZ)], axis=1)
        wide = both.astype(jnp.float32)
        some = jnp.concatenate([wide[8 * y : 8 * y + 8] for y in range(half, 24, 2)], axis=0).astype(jnp.bfloat16)
        flat = jnp.dot(lateral[half * 128 : half * 128 + 128], both, preferred_element_type=jnp.float32)
        deep = jnp.dot(some, depth[...], preferred_element_type=jnp.float32)
        return flat[0:32] + deep[64:96], flat[32:64] - deep[32:64], flat[64:96] + deep[0:32], flat[96:128]

    for half in range(2):
        batch = (2, 8)[half]
        last = panels // batch - 1

        @pl.loop(0, panels // batch)
        def _(q):
            if half == 0:
                for n in range(batch):
                    load(0, q * batch + n).wait()
                    load(1, q * batch + n).wait()
            for n in range(batch):
                k = q * batch + n
                sums = None
                for j in range(levels // 2):
                    a, a0, a1, a2 = parts(0, k, j, half)
                    b, b0, b1, b2 = parts(1, k, j, half)
                    new = (a * b, a * (b0 + b1 + b2), (a0 + a1 + a2) * b, a0 * b0 + a1 * b1 + a2 * b2)
                    sums = new if sums is None else tuple(x + y for x, y in zip(sums, new))
                image = [(total[:, :NZ] + total[:, NZ:]).reshape(shots, 8, NZ) for total in sums]
                images[:, 3 * half, k] = jnp.concatenate(image[:2], axis=1).astype(jnp.bfloat16)
                images[:, 1 + half, k] = jnp.concatenate(image[2:], axis=1).astype(jnp.bfloat16)
            if half == 0:
                @pl.when(q == last - 1)
                def _():
                    pl.semaphore_wait(barrier, expected)
                    shot_start(0, 0, panels - batch)

                @pl.when(q == last)
                def _():
                    shot_start(0, panels - batch, batch)

        if half == 0:
            pair_start(0, panels)
        else:
            shot_start(2, 0, panels)
            shot_start(3, 0, panels)
        gathered[half][s, core, 0:panels] = images[s, channel(half)]

    table_copy.wait()

    @pl.when(gathers)
    def _():
        gathered_pair[side, s, 0, 0:panels] = images[s, 1]
        for n in range(2):
            for g in range(shots):
                for a in range(2):
                    found = jnp.full((1, slots), panels, jnp.int32)
                    for k in range(panels):
                        place = (2 * (2 * pair + n) + a) * panels + k
                        found = jnp.where(slot_at == tile_slot[aperture[g, place]], k, found)
                    line = (n * shots + g) * 2 + a
                    pair_vector[line : line + 1, :] = found
        whole = pltpu.make_async_copy(pair_vector, pair_table, table_sem)
        whole.start()
        whole.wait()

    def combined(i, row):
        total = None
        for g in range(shots):
            for a in range(2):
                term = gathered[i][g, a, table[2 * g + a, row]].astype(jnp.float32)
                total = term if total is None else total + term
        return total

    def pair_combined(row):
        total = None
        for n in range(2):
            for g in range(shots):
                for a in range(2):
                    at = pair_table[(n * shots + g) * 2 + a, row]
                    term = gathered_pair[n, g, a, at].astype(jnp.float32)
                    total = term if total is None else total + term
        return total

    def pair_final(block, o):
        return pltpu.make_async_remote_copy(
            src_ref=line_pair.at[block, pl.ds(o * owned, owned)],
            dst_ref=final_in.at[pair, 1],
            send_sem=pair_send.at[block, o],
            recv_sem=final_recv.at[pair, 1],
            device_id=(s, 2 * block + o),
            device_id_type=MESH,
        )

    def relay_copy(i, block, o):
        return pltpu.make_async_remote_copy(
            src_ref=line_out.at[i, block, pl.ds(o * owned, owned)],
            dst_ref=relay_in.at[i, block, pl.ds(o * owned, owned)],
            send_sem=relay_send.at[i, block, o],
            recv_sem=relay_recv.at[i, block, o],
            device_id=(s, 2 * buddy + core),
            device_id_type=MESH,
        )

    def final_copy(i, block, o):
        c = channel(i)
        return pltpu.make_async_remote_copy(
            src_ref=line_out.at[i, block, pl.ds(o * owned, owned)],
            dst_ref=final_in.at[z // 2, c],
            send_sem=final_send.at[i, block, o],
            recv_sem=final_recv.at[z // 2, c],
            device_id=(s, 2 * block + o),
            device_id_type=MESH,
        )

    def final_wait(p, c):
        return pltpu.make_async_remote_copy(
            src_ref=line_out.at[0, 0, pl.ds(0, owned)],
            dst_ref=final_in.at[p, c],
            send_sem=final_send.at[0, 0, 0],
            recv_sem=final_recv.at[p, c],
            device_id=(s, partner),
            device_id_type=MESH,
        )

    def own_copy(i):
        return pltpu.make_async_remote_copy(
            src_ref=own_out.at[i],
            dst_ref=own_in.at[channel(i)],
            send_sem=own_send.at[i],
            recv_sem=own_recv.at[i],
            device_id=(s, partner),
            device_id_type=MESH,
        )

    def toward(block):
        return jnp.where(even, block > z, block < z)

    def arrived(i):
        for d in range(1, shots):
            for a in range(2):
                shot_wait(i, d, a).wait_recv()
        shot_wait(i, 0, 1 - core).wait_recv()

    def far(i):
        @pl.loop(0, chips)
        def _(j):
            block = jnp.where(even, chips - 1 - j, j)

            @pl.when(jnp.logical_and(toward(block), block != buddy))
            def _():
                for o in range(2):
                    for r in range(o * owned, (o + 1) * owned):
                        line_out[i, block, r] = combined(i, 2 * block * owned + r).astype(jnp.bfloat16)
                    relay_copy(i, block, o).start()

    def near_by(i):
        for o in range(2):
            for r in range(o * owned, (o + 1) * owned):
                line_out[i, buddy, r] = combined(i, 2 * buddy * owned + r).astype(jnp.bfloat16)
            final_copy(i, buddy, o).start()

    def here(i):
        for r in range(owned):
            own_out[i, r] = combined(i, (2 * z + 1 - core) * owned + r).astype(jnp.bfloat16)
        own_copy(i).start()
        for r in range(owned):
            own_in[channel(i), r] = combined(i, t * owned + r).astype(jnp.bfloat16)

    def relay(i):
        @pl.loop(0, chips)
        def _(j):
            block = jnp.where(even, j, chips - 1 - j)

            @pl.when(jnp.logical_and(block != z, jnp.logical_not(toward(block))))
            def _():
                for o in range(2):
                    relay_copy(i, block, o).wait_recv()
                    for r in range(o * owned, (o + 1) * owned):
                        total = combined(i, 2 * block * owned + r) + relay_in[i, block, r].astype(jnp.float32)
                        line_out[i, block, r] = total.astype(jnp.bfloat16)
                    final_copy(i, block, o).start()

    def finish(c):
        if c == 1:
            @pl.when(jnp.logical_and(is_hub, core == 1))
            def _():
                own_copy(0).wait_recv()
        else:
            @pl.when(foreign(c))
            def _():
                own_copy(c // 2).wait_recv()

        for p in range(chips // 2):
            if c == 1:
                @pl.when(jnp.logical_or(p != pair, jnp.logical_not(is_hub)))
                def _():
                    final_wait(p, c).wait_recv()
            else:
                final_wait(p, c).wait_recv()
        for r in range(owned):
            total = own_in[c, r].astype(jnp.float32)
            for p in range(chips // 2):
                total = total + final_in[p, c, r].astype(jnp.float32)
            near_y = slice(c // 2 * 8, c // 2 * 8 + 8)
            for kind in range(2):
                image = kind if c in (0, 3) else kind + 2
                out[r, image, near_y] = factor[(0, 1, 1, 2)[image], r, near_y] * total[kind * 8 : kind * 8 + 8]

    def gather_pair():
        for d in range(shots):
            for a in range(2):
                if d or a:
                    pair_wait(d, 0, a).wait_recv()
                    pair_wait(d, 1, a).wait_recv()
        pair_wait(0, 1 - side, 0).wait_recv()

        @pl.loop(0, chips)
        def _(j):
            block = jnp.where(even, j, chips - 1 - j)

            @pl.when(block != z)
            def _():
                for o in range(2):
                    for r in range(o * owned, (o + 1) * owned):
                        line_pair[block, r] = pair_combined(2 * block * owned + r).astype(jnp.bfloat16)
                    pair_final(block, o).start()

        for r in range(owned):
            own_out[0, r] = pair_combined((2 * z + 1) * owned + r).astype(jnp.bfloat16)
        own_copy(0).start()
        for r in range(owned):
            own_in[1, r] = pair_combined(2 * z * owned + r).astype(jnp.bfloat16)

    @pl.when(core == 1)
    def _():
        arrived(0)
        far(0)
        near_by(0)
        here(0)
        relay(0)

    near[3].wait()
    rows = pl.ds(pl.multiple_of(s * width, width), width)
    for r in range(owned):
        speed_p = model[r, 0, rows].astype(jnp.float32)
        speed_s = model[r, 1, rows].astype(jnp.float32)
        shear = model[r, 2, rows].astype(jnp.float32) * speed_s
        factor[0, r] = model[r, 2, rows].astype(jnp.float32) * speed_p
        factor[1, r] = shear
        factor[2, r] = shear * speed_s / speed_p
    pl.when(gathers)(gather_pair)
    arrived(1)
    far(1)
    near_by(1)
    here(1)
    relay(1)
    for c in range(4):
        finish(c)

    for c in (0, 2, 3):
        for d in range(1, shots):
            shot_copy(c, d, 0, panels).wait_send()

        @pl.when(foreign(c))
        def _():
            shot_copy(c, 0, 0, panels).wait_send()

    for d in range(1, shots):
        pair_copy(d, 0, panels).wait_send()

    @pl.when(jnp.logical_not(gathers))
    def _():
        pair_copy(0, 0, panels).wait_send()

    @pl.when(gathers)
    def _():
        own_copy(0).wait_send()

        @pl.loop(0, chips)
        def _(block):
            @pl.when(block != z)
            def _():
                pair_final(block, 0).wait_send()
                pair_final(block, 1).wait_send()

    def sent(i):
        own_copy(i).wait_send()

        @pl.loop(0, chips)
        def _(block):
            relayed = jnp.logical_and(toward(block), block != buddy)

            @pl.when(relayed)
            def _():
                relay_copy(i, block, 0).wait_send()
                relay_copy(i, block, 1).wait_send()

            @pl.when(jnp.logical_and(block != z, jnp.logical_not(relayed)))
            def _():
                final_copy(i, block, 0).wait_send()
                final_copy(i, block, 1).wait_send()

    pl.when(core == 1)(lambda: sent(0))
    sent(1)


def tall(array):
    lead = array.shape[:-2]
    wide = array.shape[-1] // NZ
    array = array.reshape(lead + (8, wide, NZ))
    return jnp.swapaxes(array, -3, -2).reshape(lead + (8 * wide, NZ))


def body(src_field, rcv_field, model_panels, deriv_taps, aperture, tile_slot):
    tiles = lax.axis_size("tile")
    shots = lax.axis_size("shot")
    owned = model_panels.shape[0]
    panels, levels = src_field.shape[3], src_field.shape[1]
    chips = tiles // 2
    slots = tiles * owned
    width = 64 // shots

    vmem = pl.BlockSpec(memory_space=pltpu.VMEM)
    hbm = pl.BlockSpec(memory_space=pltpu.HBM)
    line = (2, chips, 2 * owned, width, NZ)
    result = pl.pallas_call(
        functools.partial(kernel, shots, tiles),
        out_shape=pltpu.VMEM((owned, 4, width, NZ), jnp.float32),
        in_specs=[hbm] * 6,
        out_specs=vmem,
        scratch_shapes=[
            pltpu.VMEM((2, panels, levels, 3, 64, NZ), jnp.bfloat16),
            pltpu.VMEM((256, 192), jnp.bfloat16),
            pltpu.VMEM((2 * NZ, 2 * NZ), jnp.bfloat16),
            pltpu.VMEM((shots, 4, panels, width, NZ), jnp.bfloat16),
            pltpu.VMEM((shots, 2, panels + 1, width, NZ), jnp.bfloat16),
            pltpu.VMEM((shots, 2, panels + 1, width, NZ), jnp.bfloat16),
            pltpu.VMEM((2, shots, 2, panels + 1, width, NZ), jnp.bfloat16),
            pltpu.VMEM(line, jnp.bfloat16),
            pltpu.VMEM(line[1:], jnp.bfloat16),
            pltpu.VMEM(line, jnp.bfloat16),
            pltpu.VMEM((chips // 2, 4, owned, width, NZ), jnp.bfloat16),
            pltpu.VMEM((2, owned, width, NZ), jnp.bfloat16),
            pltpu.VMEM((4, owned, width, NZ), jnp.bfloat16),
            pltpu.SemaphoreType.DMA((2, panels)),
            pltpu.SemaphoreType.DMA((4, shots)),
            pltpu.SemaphoreType.DMA((2, shots, 2)),
            pltpu.SemaphoreType.DMA((shots, 2, 2)),
            pltpu.SemaphoreType.DMA((2, chips, 2)),
            pltpu.SemaphoreType.DMA((2, chips, 2)),
            pltpu.SemaphoreType.DMA((2, chips, 2)),
            pltpu.SemaphoreType.DMA((chips, 2)),
            pltpu.SemaphoreType.DMA((chips // 2, 4)),
            pltpu.SemaphoreType.DMA((2,)),
            pltpu.SemaphoreType.DMA((2,)),
            pltpu.VMEM((2 * shots, slots), jnp.int32),
            pltpu.SMEM((2 * shots, slots), jnp.int32),
            pltpu.SemaphoreType.DMA,
            pltpu.VMEM((4 * shots, slots), jnp.int32),
            pltpu.SMEM((4 * shots, slots), jnp.int32),
            pltpu.SMEM(deriv_taps.shape, jnp.float32),
            pltpu.SMEM(aperture.shape, jnp.int32),
            pltpu.SMEM(tile_slot.shape, jnp.int32),
            pltpu.VMEM((owned, 3, 64, NZ), jnp.bfloat16),
            pltpu.SemaphoreType.DMA((4,)),
            pltpu.VMEM((3, owned, width, NZ), jnp.float32),
        ],
        compiler_params=pltpu.CompilerParams(collective_id=0, has_side_effects=True, vmem_limit_bytes=48 * 1024 * 1024),
    )(*[pltpu.with_memory_space_constraint(v, pltpu.HBM) for v in (deriv_taps, aperture, tile_slot, tall(src_field[0]), tall(rcv_field[0]), tall(model_panels))])

    def spill(near, far, sem):
        copies = [pltpu.make_async_copy(near.at[r], far.at[r], sem.at[r]) for r in range(owned)]
        for copy in copies:
            copy.start()
        for copy in copies:
            copy.wait()

    wide = jnp.swapaxes(result.reshape(owned, 4, width // 8, 8, NZ), 2, 3)
    return wide.reshape(owned, 4, 8, (width // 8) * NZ)


def solution(mesh):
    return jax.shard_map(
        body,
        mesh=mesh,
        in_specs=(
            P("shot", None, None, "tile", None, None),
            P("shot", None, None, "tile", None, None),
            P("tile", None, None, None),
            P(),
            P(),
            P(),
        ),
        out_specs=P("tile", None, None, "shot"),
        check_vma=False,
    )
```
